32 devices in a mesh: site: 2 (over y), pt: 4 (over z), var: 2 (over x), cmp: 2 (over core).
Axes of the slice: x: 2, y: 2, z: 4, core: 2. Of those that a mesh axis runs over, the one named last changes fastest.
Arguments:
- strain_green: bfloat16 [5120, 24, 256], P(('site', 'pt'), None, 'cmp'), parts along dimension 0, may hold values from -2.390625 to 2.390625
- green_scale: float32 [40, 24], P(('site', 'pt')), parts along dimension 0, may hold values from 0.3 to 3
- mechanism: float32 [6, 2560], P(None, 'pt'), may hold values from -4 to 4
- slip_amplitude: bfloat16 [4, 32, 1536], P('pt', 'var'), may hold values from 0.19921875 to 2
- onset_time: float32 [4, 32, 1536], P('pt', 'var'), may hold values from 0 to 128
- rupture_row: int32 [4], replicated, may hold values from 0 to 3, each once
- rupture_blocks: int32 [4, 12], replicated, may hold values from 0 to 19, as said below
- block_count: int32 [4], replicated, may hold values from 1 to 12, 16 in all
- crossover: int32 [4], replicated, may hold values from 128 to 251
- high_band: float32 [8, 32, 2, 512], P(('site', 'pt'), 'var', None, 'cmp'), parts along dimension 0, may hold values from -6 to 6
Outputs:
- seismograms: float32 [8, 32, 2, 512], P(('site', 'pt'), 'var', None, 'cmp'), parts along dimension 0
The draws below stay inside these ranges and needn't reach their ends.
There are 2 independent parts, one for each index of `site`. The reference program is written for one: setup_inputs(seed, part) draws one part's arguments, and reference() takes and returns one part's arrays. A program takes and returns all parts, laid end to end along the dimension named above; an argument that names none is the same for every part. Nothing has to cross between parts.
Inputs may be any that keep to these rules, and one draw needn't show every extreme that they name: `rupture_blocks`: each row names 12 different point blocks; rupture r covers the first block_count[r] of them.
All inputs are finite; a program needn't handle non-finite values.
Results may differ from the reference program's by a relative error of at most 0.0028.
Values may be sent and summed in bfloat16 or wider, within the bound.
A program may use at most 64 MiB of HBM per device.

```python
import math
import jax
import jax.numpy as jnp
import numpy as np
from jax import lax

BINS = 256
SAMPLES = 512
BLOCK = 128
MAXB = 12
NBLOCKS = 20
NPTS = 2560
RUPTURES = 4
VARS = 32


def draw_rupture_blocks(key, part):
    row_keys = jax.random.split(key, RUPTURES)
    shuffled = jax.vmap(lambda row_key: jax.random.permutation(row_key, NBLOCKS))(row_keys)
    return shuffled[:, :MAXB].astype(jnp.int32)


def plant(drawn, key, least, top_value):
    longest = drawn.shape.index(max(drawn.shape))
    spots = []
    for shift in (0, 1):
        where = [jax.random.randint(jax.random.fold_in(key, axis), (), 0, length) for axis, length in enumerate(drawn.shape)]
        where[longest] = (where[longest] + shift) % drawn.shape[longest]
        spots.append(tuple(where))
    return drawn.at[spots[0]].set(least).at[spots[1]].set(top_value)


def block_scale(rng, extent, shards, smallest, top_value):
    def one(dim, shards_of):
        draws = jax.random.uniform(jax.random.fold_in(jax.random.fold_in(rng, 6), dim), (shards_of,), jnp.float32, smallest / len(shards), top_value / len(shards))
        return jnp.repeat(jnp.exp(draws), extent[dim] // shards_of).reshape((-1,) + (1,) * (len(extent) - dim - 1))

    loudness = one(*shards[0])
    for cut in shards[1:]:
        loudness = loudness * one(*cut)
    return loudness


def profile(count, total, most, slope):
    portions = [(1 << 20) // math.isqrt(grade ** slope) + 1 for grade in range(2, count + 1)]
    rest, holding = total - most - (count - 1), [1] * (count - 1)
    while rest > 0:
        movable = [i for i in range(count - 1) if holding[i] < most]
        whole, remaining = sum([portions[i] for i in movable]), rest
        for i in movable:
            extra = min(most - holding[i], max(1, remaining * portions[i] // whole), rest)
            holding[i] = holding[i] + extra
            rest = rest - extra
    return np.array([most] + holding)


def uneven_parts(own_key, number_of, total, limit, lean):
    if number_of == 2:
        one = jax.random.randint(own_key, (), max(1, total - limit), min(limit, total - 1) + 1)
        return jnp.stack([one, total - one])
    sizes = jnp.asarray(profile(number_of, total, limit, lean), jnp.int32)
    couples = (number_of - 1) // 2
    source_of, receiver = sizes[1:1 + 2 * couples:2], sizes[2:2 + 2 * couples:2]
    slack = jnp.minimum(source_of - 1, limit - receiver)
    moved = jax.random.randint(jax.random.fold_in(own_key, 1), (couples,), 0, 1 << 20) % (slack + 1)
    sizes = sizes.at[1:1 + 2 * couples:2].set(source_of - moved).at[2:2 + 2 * couples:2].set(receiver + moved)
    return sizes[jax.random.permutation(jax.random.fold_in(own_key, 2), number_of)]


def centred(stream_key, extent, scale, limit, cuts=(), dtype=jnp.bfloat16):
    level = block_scale(stream_key, extent, cuts, -0.22, 0.18) if cuts else 1.0
    entries = jax.random.normal(stream_key, extent, jnp.float32) * scale * level
    return jnp.minimum(jnp.maximum(entries, -limit), limit).astype(dtype)


def setup_inputs(seed: int = 0, part: int = 0) -> dict:
    splits = jax.random.split(jax.random.key(seed), 11)
    part_splits = jax.random.split(jax.random.fold_in(splits[10], part), 11)
    return {
        "strain_green": centred(part_splits[0], (NPTS, 24, BINS), 0.3, 2.390625, ((0, 4), (2, 2))),
        "green_scale": jnp.clip(jnp.exp(math.log(3.0) - 2.3025851 * jax.random.uniform(part_splits[1], (NBLOCKS, 24), jnp.float32) ** block_scale(part_splits[1], (NBLOCKS, 24), ((0, 4),), -0.2, 0.2)), 0.3, 3.0),
        "mechanism": centred(splits[2], (6, NPTS), 1.0, 4.0, ((1, 4),), jnp.float32),
        "slip_amplitude": jnp.clip(jnp.exp(math.log(2.0) - 2.306499 * jax.random.uniform(splits[3], (RUPTURES, VARS, MAXB * BLOCK), jnp.float32) ** block_scale(splits[3], (RUPTURES, VARS, MAXB * BLOCK), ((0, 4), (1, 2)), -0.2, 0.2)), 0.19921875, 2.0).astype(jnp.bfloat16),
        "onset_time": jnp.clip(128.0 * jax.random.uniform(splits[4], (RUPTURES, VARS, MAXB * BLOCK), jnp.float32) ** block_scale(splits[4], (RUPTURES, VARS, MAXB * BLOCK), ((0, 4), (1, 2)), -0.2, 0.2), 0.0, 128.0),
        "rupture_row": jax.random.permutation(splits[5], RUPTURES).astype(jnp.int32),
        "rupture_blocks": draw_rupture_blocks(jax.random.fold_in(splits[10], 71), part),
        "block_count": uneven_parts(splits[7], RUPTURES, RUPTURES * (MAXB // 3), MAXB, 2).astype(jnp.int32),
        "crossover": plant(jax.random.randint(splits[8], (RUPTURES,), BINS // 2, BINS - 4), jax.random.fold_in(splits[8], 1), BINS // 2, (BINS - 4) - 1).astype(jnp.int32),
        "high_band": centred(part_splits[9], (RUPTURES, VARS, 2, SAMPLES), 1.0, 6.0, ((0, 4), (1, 2), (3, 2)), jnp.float32),
    }


taper_width = 8.0


def green_tensor(strain_green, green_scale, mechanism):
    points = strain_green.shape[0]
    bins_here = strain_green.shape[2]
    blocks_scale = jnp.repeat(green_scale, points // green_scale.shape[0], axis=0)
    factors = blocks_scale.reshape(points, 4, 6) * jnp.transpose(mechanism)[:, None, :]
    spectra = strain_green.reshape(points, 4, 6, bins_here).astype(jnp.float32)
    summed = jnp.einsum("pkjf,pkj->pkf", spectra, factors, precision=lax.Precision.HIGHEST)
    return summed.astype(jnp.bfloat16)


def block_term(green_block, amplitude, onset_block, phase_step):
    angles = onset_block[:, :, None] * phase_step[None, None, :]
    weight = amplitude.astype(jnp.float32)[:, :, None]
    with_cos = weight * jnp.cos(angles)
    with_sin = weight * jnp.sin(angles)
    green_wide = green_block.astype(jnp.float32)
    real_green = green_wide[:, 0:2]
    imag_green = green_wide[:, 2:4]
    highest = lax.Precision.HIGHEST
    real_part = jnp.einsum("vqf,qcf->vcf", with_cos, real_green, precision=highest) + jnp.einsum("vqf,qcf->vcf", with_sin, imag_green, precision=highest)
    imag_part = jnp.einsum("vqf,qcf->vcf", with_cos, imag_green, precision=highest) - jnp.einsum("vqf,qcf->vcf", with_sin, real_green, precision=highest)
    return jnp.concatenate([real_part, imag_part], axis=1)


def reference(strain_green, green_scale, mechanism, slip_amplitude, onset_time, rupture_row, rupture_blocks, block_count, crossover, high_band):
    highest = lax.Precision.HIGHEST
    green = green_tensor(strain_green, green_scale, mechanism)
    frequency = jnp.arange(BINS).astype(jnp.float32)
    phase_step = frequency * (2.0 * math.pi / SAMPLES)

    def one_row(position):
        rupture = rupture_row[position]
        blocks = rupture_blocks[rupture]
        covered = block_count[rupture]
        amplitudes = slip_amplitude[position]
        onsets = onset_time[position]

        def visit(running, slot_number):
            first_point = (blocks[slot_number] * BLOCK).astype(jnp.int32)
            green_block = lax.dynamic_slice_in_dim(green, first_point, BLOCK, 0)
            offset = (slot_number * BLOCK).astype(jnp.int32)
            amplitude = lax.dynamic_slice_in_dim(amplitudes, offset, BLOCK, 1)
            onset_block = lax.dynamic_slice_in_dim(onsets, offset, BLOCK, 1)
            contribution = block_term(green_block, amplitude, onset_block, phase_step)
            return running + jnp.where(slot_number < covered, contribution, jnp.zeros_like(contribution)), None

        running, unused = lax.scan(visit, jnp.zeros((VARS, 4, BINS), jnp.float32), jnp.arange(MAXB).astype(jnp.int32))
        return running

    spectrum = lax.map(one_row, jnp.arange(RUPTURES).astype(jnp.int32))
    samples_index = jnp.arange(SAMPLES).astype(jnp.int32)
    bins_index = jnp.arange(BINS).astype(jnp.int32)
    angles = ((bins_index[:, None] * samples_index[None, :]) % SAMPLES).astype(jnp.float32) * (2.0 * math.pi / SAMPLES)
    cosine = jnp.cos(angles)
    sine_table = jnp.sin(angles)
    band_rows = high_band.reshape(-1, SAMPLES)
    band_real = jnp.dot(band_rows, cosine.T, precision=highest)
    band_imag = -jnp.dot(band_rows, sine_table.T, precision=highest)
    crossing = crossover[rupture_row].astype(jnp.float32)
    taper_weight = jnp.clip((crossing[:, None] - frequency[None, :]) / taper_width + 0.5, 0.0, 1.0)
    taper_rows = jnp.repeat(taper_weight, VARS * 2, axis=0)
    spectrum_real = spectrum[:, :, 0:2].reshape(-1, BINS)
    spectrum_imag = spectrum[:, :, 2:4].reshape(-1, BINS)
    coefficient = jnp.where(bins_index == 0, 1.0, 2.0) / SAMPLES
    excess_real = taper_rows * (spectrum_real - band_real) * coefficient
    excess_imag = taper_rows * (spectrum_imag - band_imag) * coefficient
    basis_table = jnp.concatenate([cosine, -sine_table], axis=0)
    low_band = jnp.dot(jnp.concatenate([excess_real, excess_imag], axis=1), basis_table, precision=highest)
    return (band_rows + low_band).reshape(high_band.shape)
```

```python
import functools
import math

import jax
import jax.numpy as jnp
import numpy as np
from jax import lax
from jax.experimental import pallas as pl
from jax.experimental.pallas import tpu as pltpu
from jax.sharding import PartitionSpec as P

taper_width = 8.0
onset_middle = 64.0
onset_steps = 512.0
slip_steps = 1024.0
MESH = pl.DeviceIdType.MESH
VMEM = pltpu.VMEM
SMEM = pltpu.SMEM


def column_bins(bins_here):
    half = bins_here // 2
    column = np.arange(2 * bins_here)
    return (column // bins_here) * half + column % half, (column // half) % 2


def basis_tables(bins_here, parts, samples):
    bins, imaginary = column_bins(bins_here)
    time = np.arange(samples)[:, None]
    tables = []
    for part in range(parts):
        angle = ((part * bins_here + bins)[None, :] * time % samples) * (2.0 * math.pi / samples)
        tables.append(np.where(imaginary[None, :] == 1, -np.sin(angle), np.cos(angle)))
    exact = np.stack(tables)
    upper = exact.astype(jnp.bfloat16)
    lower = (exact - upper.astype(np.float64)).astype(jnp.bfloat16)
    return np.stack([upper, lower], axis=1)


def spread_tables(parts_of, terms, group):
    depth = group * parts_of
    column = np.arange(depth)
    spread = (np.arange(parts_of)[:, None] == column[None, :] % parts_of).astype(jnp.bfloat16)
    quarter = np.arange(parts_of // terms * group)
    own_point = quarter[:, None] % group == column[None, :] // parts_of
    own_term = quarter[:, None] // group == (column[None, :] % parts_of) // terms
    return spread, (own_point & own_term).astype(jnp.bfloat16)


def wide_dot(rows, upper, lower, dims):
    head = rows.astype(jnp.bfloat16)
    tail = (rows - head.astype(jnp.float32)).astype(jnp.bfloat16)
    dot = functools.partial(
        lax.dot_general, dimension_numbers=(dims, ((), ())), preferred_element_type=jnp.float32
    )
    return dot(head, upper) + (dot(head, lower) + dot(tail, upper))


def hail(peers):
    barrier = pltpu.get_barrier_semaphore()
    for peer in peers:
        pl.semaphore_signal(barrier, inc=1, device_id=peer, device_id_type=MESH)


def await_all(peers):
    pl.semaphore_wait(pltpu.get_barrier_semaphore(), len(peers))


def greet(peers):
    hail(peers)
    await_all(peers)


def others(me, count):
    return [{"pt": lax.rem(me + step, count)} for step in range(1, count)]


def gather_kernel(
    count,
    row_ref,
    blocks_ref,
    covered_ref,
    crossover_ref,
    strain_ref,
    scale_hbm,
    mechanism_hbm,
    slip_hbm,
    onset_hbm,
    band_hbm,
    table_hbm,
    spread_ref,
    own_ref,
    weights_ref,
    slots_ref,
    band_both,
    table_ref,
    weight_ref,
    scale_ref,
    mechanism_ref,
    slip_ref,
    onset_ref,
    band_ref,
    strain_buf,
    coded_ref,
    slot_pack,
    local_sem,
    load_sem,
    strain_sem,
    send_sem,
    recv_sem,
    pass_sem,
    passed_sem,
):
    me = lax.axis_index("pt")
    part = lax.axis_index("cmp")
    partner = {"cmp": 1 - part}
    blocks_here = scale_ref.shape[0]
    parts_of = scale_ref.shape[1]
    stretch = strain_ref.shape[0] // blocks_here
    block = stretch // parts_of
    bins = strain_ref.shape[1]
    half = bins // 2
    own = band_ref.shape[3]
    variations = band_ref.shape[1]
    samples = own * table_ref.shape[0]
    peers = others(me, count)
    hail(peers + [partner])
    loads = []
    for k, (source, target) in enumerate(
        (
            (slip_hbm, slip_ref),
            (onset_hbm, onset_ref),
            (band_hbm, band_ref),
            (mechanism_hbm, mechanism_ref),
            (scale_hbm, scale_ref),
        )
    ):
        copy = pltpu.make_async_copy(source, target, load_sem.at[k])
        copy.start()
        loads.append(copy)
    def strain_rows(b):
        return strain_ref.at[pl.ds(pl.multiple_of(b * stretch, stretch), stretch)]

    for b in range(blocks_here):
        pltpu.make_async_copy(strain_rows(b), strain_buf.at[pl.ds(b * stretch, stretch)], strain_sem.at[b]).start()
    table_copy = pltpu.make_async_copy(table_hbm, table_ref, local_sem)
    table_copy.start()
    loads[0].wait()
    loads[1].wait()
    rupture = row_ref[me]
    covered = covered_ref[rupture]
    spread = variations // 2

    slot_total = blocks_ref.shape[1]

    def chosen(target):
        lowest = target * blocks_here
        slots = [jnp.int32(0)] * blocks_here
        found = jnp.int32(0)
        for slot in range(slot_total):
            named = blocks_ref[rupture, slot]
            live = (slot < covered) & (named >= lowest) & (named < lowest + blocks_here)
            for k in range(min(blocks_here, slot + 1)):
                slots[k] = jnp.where(live & (found == k), slot, slots[k])
            found = found + live.astype(jnp.int32)
        return slots

    for slot in range(slot_total):
        lanes = pl.ds(slot * block, block)
        onset = (onset_ref[0, :, lanes] - onset_middle) * onset_steps
        onset = jnp.minimum(jnp.round(onset), onset_middle * onset_steps - 1.0)
        slip = slip_ref[0, :, lanes].astype(jnp.float32) * slip_steps
        for h in range(2):
            lines = slice(h * spread, (h + 1) * spread)
            coded_ref[h, slot] = (
                jnp.concatenate([onset[lines], slip[lines]], axis=0)
                .astype(jnp.int32)
                .astype(coded_ref.dtype)
            )

    def pack(step, carry):
        for k, slot in enumerate(chosen(lax.rem(me + 1 + step, count))):
            slot_pack[step, k] = coded_ref[part, slot]
        return carry

    lax.fori_loop(0, count - 1, pack, 0)
    await_all(peers + [partner])
    sends = []
    for step, peer in enumerate(peers):
        copy = pltpu.make_async_remote_copy(
            src_ref=slot_pack.at[step],
            dst_ref=slots_ref.at[me, part],
            send_sem=send_sem.at[step],
            recv_sem=recv_sem.at[step],
            device_id=peer,
            device_id_type=MESH,
        )
        copy.start()
        sends.append(copy)
    loads[2].wait()
    for c in range(2):
        band_both[0, pl.ds(c * variations, variations), :] = band_ref[0, :, c, :]
    band_copy = pltpu.make_async_remote_copy(
        src_ref=band_both.at[0],
        dst_ref=band_both.at[1],
        send_sem=send_sem.at[count - 1],
        recv_sem=recv_sem.at[count - 1],
        device_id=partner,
        device_id_type=MESH,
    )
    band_copy.start()
    for k, slot in enumerate(chosen(me)):
        for h in range(2):
            slots_ref[me, h, k] = coded_ref[h, slot]

    crossing = crossover_ref[rupture].astype(jnp.float32)
    column = lax.broadcasted_iota(jnp.int32, weight_ref.shape, 1)
    frequency_id = part * bins + (column // bins) * half + column % half
    frequency = frequency_id.astype(jnp.float32)
    taper = jnp.clip((crossing - frequency) / taper_width + 0.5, 0.0, 1.0)
    weight_ref[...] = taper * jnp.where(frequency_id == 0, 1.0, 2.0) / samples
    loads[3].wait()
    loads[4].wait()
    group = 8
    pair = 2 * group
    depth = group * parts_of
    low_lanes = lax.broadcasted_iota(jnp.int32, (pair, bins), 1) < half
    dot = functools.partial(jnp.dot, preferred_element_type=jnp.float32)

    def make_block(b, carry):
        pltpu.make_async_copy(strain_rows(b), strain_buf.at[pl.ds(b * stretch, stretch)], strain_sem.at[b]).wait()
        moment = mechanism_ref[:, pl.ds(pl.multiple_of(b * block, block), block)]
        factors = jnp.transpose(jnp.concatenate([moment] * 4, axis=0)) * scale_ref[pl.ds(b, 1), :]
        head = factors.astype(jnp.bfloat16)
        tail = (factors - head.astype(jnp.float32)).astype(jnp.bfloat16)
        wide = [dot(piece, spread_ref[...]) for piece in (head, tail)]
        for first in range(0, block, pair):
            sums = []
            for start in (first, first + group):
                rows = []
                for piece in wide:
                    tile = piece[start : start + group]
                    twice = jnp.concatenate([tile, tile], axis=0).astype(jnp.bfloat16)
                    rows += [twice * own_ref[:pair], twice * own_ref[pair:]]
                product = dot(
                    jnp.concatenate(rows, axis=0),
                    strain_buf[pl.ds(pl.multiple_of(b * stretch + start * parts_of, depth), depth), :],
                )
                sums.append(product[: 2 * pair] + product[2 * pair :])
            quarters = [
                jnp.concatenate([part_sum[q * group : (q + 1) * group] for part_sum in sums], axis=0)
                for q in range(4)
            ]
            for c in range(2):
                real, imag = quarters[c], quarters[2 + c]
                real_turned = pltpu.roll(real, half, 1)
                imag_turned = pltpu.roll(imag, half, 1)
                lanes = pl.ds(c * bins, bins)
                pieces = (
                    (0, 0, real, imag_turned),
                    (0, 1, imag, -real_turned),
                    (1, 0, real_turned, imag),
                    (1, 1, imag_turned, -real),
                )
                for which, lower, first_half, second_half in pieces:
                    weights_ref[b, which, pl.ds(lower * block + first, pair), lanes] = jnp.where(
                        low_lanes, first_half, second_half
                    ).astype(jnp.bfloat16)
        return carry

    lax.fori_loop(0, blocks_here, make_block, 0)

    passes = []
    for step in range(count - 1):
        source_row = lax.rem(me + count - 1 - step, count)
        sends[step].wait_recv()
        held = slots_ref.at[source_row, part]
        copy = pltpu.make_async_remote_copy(
            src_ref=held,
            dst_ref=held,
            send_sem=pass_sem.at[step],
            recv_sem=passed_sem.at[step],
            device_id=partner,
            device_id_type=MESH,
        )
        copy.start()
        passes.append(copy)
    table_copy.wait()
    band_copy.wait()
    for copy in sends:
        copy.wait_send()
    for copy in passes:
        copy.wait()


def turn(first, second):
    return (
        first[0] * second[0] - first[1] * second[1],
        first[0] * second[1] + first[1] * second[0],
    )


def quarter_unit(angle):
    off = angle - 0.25 * math.pi
    square = off * off
    sine = off * (
        1.0
        + square * (-1.0 / 6 + square * (1.0 / 120 + square * (-1.0 / 5040 + square * (1.0 / 362880))))
    )
    cosine = 1.0 + square * (
        -0.5
        + square
        * (1.0 / 24 + square * (-1.0 / 720 + square * (1.0 / 40320 + square * (-1.0 / 3628800))))
    )
    scale = math.sqrt(0.5)
    return scale * (cosine - sine), scale * (cosine + sine)


def slot_rows(slots_ref, row, found, spread):
    pieces = [
        slots_ref[row, h, found].astype(jnp.int32).astype(jnp.float32)
        for h in range(slots_ref.shape[1])
    ]
    onset = jnp.concatenate([piece[:spread] for piece in pieces], axis=0)
    slip = jnp.concatenate([piece[spread:] for piece in pieces], axis=0)
    return onset / onset_steps + onset_middle, slip / slip_steps


def pair_spectrum(step_angle, slots_ref, weights_ref, row, found, local):
    halves, depth, columns = weights_ref.shape[1:]
    spread = slots_ref.shape[3] // 2
    bins = columns // 2
    half = bins // 2
    fine_total = 16
    reach = fine_total // 2
    onset, slip = slot_rows(slots_ref, row, found, spread)
    variations = onset.shape[0]
    powers = [None, quarter_unit(step_angle * onset)]
    for k in range(2, reach + 1):
        powers.append(turn(powers[k // 2], powers[k - k // 2]))
    leap = turn(powers[reach], powers[reach])
    far = leap
    for unused in range(int(math.log2(bins // fine_total))):
        far = turn(far, far)
    second_part = lax.axis_index("cmp") == 1
    centre = turn(
        powers[reach],
        (slip * jnp.where(second_part, far[0], 1.0), slip * jnp.where(second_part, far[1], 0.0)),
    )
    lane_bin = lax.broadcasted_iota(jnp.int32, (8, 128), 1) % half
    spectra = []
    for which in range(halves):
        pieces = []
        for h in range(half // fine_total):
            near = [None] * fine_total
            near[reach] = centre
            for k in range(1, reach + 1):
                cos_cos, sin_sin = centre[0] * powers[k][0], centre[1] * powers[k][1]
                sin_cos, cos_sin = centre[1] * powers[k][0], centre[0] * powers[k][1]
                near[reach - k] = (cos_cos + sin_sin, sin_cos - cos_sin)
                if k < reach:
                    near[reach + k] = (cos_cos - sin_sin, sin_cos + cos_sin)
            pieces += [
                jnp.concatenate([phase[0].astype(jnp.bfloat16), phase[1].astype(jnp.bfloat16)], axis=1)
                for phase in near
            ]
            centre = turn(centre, leap)
        product = jnp.dot(
            jnp.concatenate(pieces, axis=0),
            weights_ref[local, which],
            preferred_element_type=jnp.float32,
        )
        tiles = [
            [jnp.zeros((8, 128), jnp.float32) for lane in range(columns // 128)]
            for line in range(variations // 8)
        ]
        for k in range(half):
            here = lane_bin == k
            for line, across in enumerate(tiles):
                start = k * variations + 8 * line
                for lane in range(len(across)):
                    across[lane] = jnp.where(
                        here, product[start : start + 8, 128 * lane : 128 * (lane + 1)], across[lane]
                    )
        spectra.append(
            jnp.concatenate([jnp.concatenate(across, axis=1) for across in tiles], axis=0)
        )
    return spectra


def pair_kernel(
    step_angle,
    row_ref,
    blocks_ref,
    covered_ref,
    weights_ref,
    slots_ref,
    total_ref,
    codes_ref,
):
    me = lax.axis_index("pt")
    blocks_here = weights_ref.shape[0]
    rows = slots_ref.shape[0]
    later = codes_ref.shape[0]
    lowest = me * blocks_here
    total_ref[...] = jnp.zeros_like(total_ref)
    codes_ref[...] = jnp.full(codes_ref.shape, -1, jnp.int32)

    def one_row(row, seen):
        rupture = row_ref[row]

        def one_slot(slot, carry):
            found, seen = carry
            local = blocks_ref[rupture, slot] - lowest
            live = (local >= 0) & (local < blocks_here)

            @pl.when(live & (seen < later))
            def _():
                code = (row * blocks_here + local) * blocks_here + found
                codes_ref[pl.ds(seen, 1)] = jnp.full((1,) + codes_ref.shape[1:], code, jnp.int32)

            @pl.when(live & (seen >= later))
            def _():
                spectra = pair_spectrum(step_angle, slots_ref, weights_ref, row, found, local)
                for which, spectrum in enumerate(spectra):
                    total_ref[row, which] += spectrum

            return found + live.astype(jnp.int32), seen + live.astype(jnp.int32)

        return lax.fori_loop(0, covered_ref[rupture], one_slot, (jnp.int32(0), seen))[1]

    lax.fori_loop(0, rows, one_row, jnp.int32(0))


def merge_kernel(
    count,
    step_angle,
    begun_ref,
    codes_ref,
    slots_ref,
    weights_ref,
    weight_ref,
    band_ref,
    table_ref,
    excess_ref,
    total_ref,
    partial_ref,
    arrived,
    excess_send,
    send_sem,
    recv_sem,
):
    me = lax.axis_index("pt")
    part = lax.axis_index("cmp")
    partner = {"cmp": 1 - part}
    blocks_here = weights_ref.shape[0]
    rows, halves, variations, columns = begun_ref.shape
    bins = columns // 2
    own = band_ref.shape[2]
    peers = others(me, count)
    hail(peers + [partner])
    total_ref[...] = begun_ref[...]
    for j in range(codes_ref.shape[0]):
        code = codes_ref[j, 0, 0]
        safe = jnp.maximum(code, 0)
        holder = lax.div(safe, blocks_here)
        row = lax.div(holder, blocks_here)
        spectra = pair_spectrum(
            step_angle, slots_ref, weights_ref, row, safe - holder * blocks_here, holder - row * blocks_here
        )
        chosen = jnp.where(code < 0, -1, row)
        for other in range(rows):
            share = jnp.where(chosen == other, 1.0, 0.0)
            for which in range(halves):
                total_ref[other, which] += share * spectra[which]
    partial_ref[...] = total_ref[...].astype(partial_ref.dtype)
    await_all(peers + [partner])
    sends = []
    for step, peer in enumerate(peers):
        copy = pltpu.make_async_remote_copy(
            src_ref=partial_ref.at[peer["pt"]],
            dst_ref=arrived.at[step],
            send_sem=send_sem.at[step],
            recv_sem=recv_sem.at[step],
            device_id=peer,
            device_id_type=MESH,
        )
        copy.start()
        sends.append(copy)
    weight = jnp.concatenate([weight_ref[...]] * 2, axis=0)
    down = ((1,), (0,))
    spectrum = None
    for which in range(2):
        source = lax.rem(part + which, 2)
        steps = pl.ds(pl.multiple_of(source * own, own), own)
        share = wide_dot(band_ref[which], table_ref[part, 0, steps, :], table_ref[part, 1, steps, :], down)
        spectrum = share if spectrum is None else spectrum + share
    total = total_ref[me]
    for step, copy in enumerate(sends):
        copy.wait_recv()
        total = total + arrived[step].astype(jnp.float32)
    whole = jnp.concatenate(
        [
            jnp.concatenate([total[which][:, c * bins : (c + 1) * bins] for which in range(halves)], axis=1)
            for c in range(2)
        ],
        axis=0,
    )
    excess_send[...] = (whole - spectrum) * weight
    exchange = pltpu.make_async_remote_copy(
        src_ref=excess_send,
        dst_ref=excess_ref.at[1],
        send_sem=send_sem.at[count - 1],
        recv_sem=recv_sem.at[count - 1],
        device_id=partner,
        device_id_type=MESH,
    )
    exchange.start()
    excess_ref[0] = excess_send[...]
    for copy in sends:
        copy.wait_send()
    exchange.wait()


def final_kernel(excess_ref, band_ref, table_ref, out_ref):
    part = lax.axis_index("cmp")
    variations = out_ref.shape[1]
    own = out_ref.shape[3]
    across = ((1,), (1,))
    low = band_ref[0]
    steps = pl.ds(pl.multiple_of(part * own, own), own)
    for which in range(2):
        source = lax.rem(part + which, 2)
        low = low + wide_dot(
            excess_ref[which], table_ref[source, 0, steps, :], table_ref[source, 1, steps, :], across
        )
    for c in range(2):
        out_ref[0, :, c, :] = low[c * variations : (c + 1) * variations]


def stay(array):
    return pltpu.with_memory_space_constraint(array, VMEM)


def body(
    strain_green,
    green_scale,
    mechanism,
    slip_amplitude,
    onset_time,
    rupture_row,
    rupture_blocks,
    block_count,
    crossover,
    high_band,
):
    points, parts_of, bins = strain_green.shape
    blocks_here = green_scale.shape[0]
    block = points // blocks_here
    rows_here, variations, slots = slip_amplitude.shape
    count = lax.axis_size("pt")
    parts = lax.axis_size("cmp")
    own = high_band.shape[3]
    samples = own * parts
    rows = rows_here * count
    tables = jnp.asarray(basis_tables(bins, parts, samples))
    spread, own_terms = spread_tables(parts_of, mechanism.shape[0], 8)
    vmem = pl.BlockSpec(memory_space=VMEM)
    smem = pl.BlockSpec(memory_space=SMEM)
    anywhere = pl.BlockSpec(memory_space=pltpu.HBM)
    grant = 24 * 1024 * 1024
    later = 4
    step_angle = 2.0 * math.pi / samples
    share = (blocks_here, variations, block)
    weights, slots_all, bands, table, weight = pl.pallas_call(
        functools.partial(gather_kernel, count),
        out_shape=(
            VMEM((blocks_here, 2, 2 * block, 2 * bins), jnp.bfloat16),
            VMEM((rows, 2) + share, jnp.int16),
            VMEM((2, 2 * variations, own), jnp.float32),
            VMEM(tables.shape, jnp.bfloat16),
            VMEM((variations, 2 * bins), jnp.float32),
        ),
        in_specs=[smem] * 4 + [anywhere] * 7 + [vmem] * 2,
        out_specs=(vmem,) * 5,
        scratch_shapes=[
            VMEM(green_scale.shape, green_scale.dtype),
            VMEM(mechanism.shape, mechanism.dtype),
            VMEM(slip_amplitude.shape, slip_amplitude.dtype),
            VMEM(onset_time.shape, onset_time.dtype),
            VMEM(high_band.shape, high_band.dtype),
            VMEM((points * parts_of, bins), strain_green.dtype),
            VMEM((2, slots // block, variations, block), jnp.int16),
            VMEM((count - 1,) + share, jnp.int16),
            pltpu.SemaphoreType.DMA,
            pltpu.SemaphoreType.DMA((5,)),
            pltpu.SemaphoreType.DMA((blocks_here,)),
            pltpu.SemaphoreType.DMA((count,)),
            pltpu.SemaphoreType.DMA((count,)),
            pltpu.SemaphoreType.DMA((count - 1,)),
            pltpu.SemaphoreType.DMA((count - 1,)),
        ],
        compiler_params=pltpu.CompilerParams(collective_id=0, has_side_effects=True),
        name="gather",
    )(
        rupture_row,
        rupture_blocks,
        block_count,
        crossover,
        strain_green.reshape(points * parts_of, bins),
        green_scale,
        mechanism,
        slip_amplitude,
        onset_time,
        high_band,
        tables,
        jnp.asarray(spread),
        jnp.asarray(own_terms),
    )
    begun, codes = pl.pallas_call(
        functools.partial(pair_kernel, step_angle),
        out_shape=(
            VMEM((rows, 2, variations, 2 * bins), jnp.float32),
            VMEM((later, 8, 128), jnp.int32),
        ),
        in_specs=[smem, smem, smem, vmem, vmem],
        out_specs=(vmem, vmem),
        compiler_params=pltpu.CompilerParams(vmem_limit_bytes=grant),
        name="pairs",
    )(rupture_row, rupture_blocks, block_count, stay(weights), stay(slots_all))
    excess = pl.pallas_call(
        functools.partial(merge_kernel, count, step_angle),
        out_shape=VMEM((2, 2 * variations, 2 * bins), jnp.float32),
        in_specs=[vmem] * 7,
        out_specs=vmem,
        scratch_shapes=[
            VMEM((rows, 2, variations, 2 * bins), jnp.float32),
            VMEM((rows, 2, variations, 2 * bins), jnp.bfloat16),
            VMEM((count - 1, 2, variations, 2 * bins), jnp.bfloat16),
            VMEM((2 * variations, 2 * bins), jnp.float32),
            pltpu.SemaphoreType.DMA((count,)),
            pltpu.SemaphoreType.DMA((count,)),
        ],
        compiler_params=pltpu.CompilerParams(collective_id=1, has_side_effects=True, vmem_limit_bytes=grant),
        name="merge",
    )(stay(begun), stay(codes), stay(slots_all), stay(weights), stay(weight), stay(bands), stay(table))
    return pl.pallas_call(
        final_kernel,
        out_shape=jax.ShapeDtypeStruct(high_band.shape, high_band.dtype),
        in_specs=[vmem, vmem, vmem],
        out_specs=vmem,
        compiler_params=pltpu.CompilerParams(vmem_limit_bytes=grant),
        name="final",
    )(stay(excess), stay(bands), stay(table))


def solution(mesh):
    return jax.shard_map(
        body,
        mesh=mesh,
        in_specs=(
            P(("site", "pt"), None, "cmp"),
            P(("site", "pt"), None),
            P(None, "pt"),
            P("pt", "var", None),
            P("pt", "var", None),
            P(),
            P(),
            P(),
            P(),
            P(("site", "pt"), "var", None, "cmp"),
        ),
        out_specs=P(("site", "pt"), "var", None, "cmp"),
        check_vma=False,
    )
```

```python
import functools
import math

import jax
import jax.numpy as jnp
import numpy as np
from jax import lax
from jax.experimental import pallas as pl
from jax.experimental.pallas import tpu as pltpu
from jax.sharding import PartitionSpec as P

taper_width = 8.0
onset_middle = 64.0
onset_steps = 512.0
slip_steps = 1024.0
MESH = pl.DeviceIdType.MESH
VMEM = pltpu.VMEM
SMEM = pltpu.SMEM


def column_bins(bins_here):
    half = bins_here // 2
    column = np.arange(2 * bins_here)
    return (column // bins_here) * half + column % half, (column // half) % 2


def basis_tables(bins_here, parts, samples):
    bins, imaginary = column_bins(bins_here)
    time = np.arange(samples)[:, None]
    tables = []
    for part in range(parts):
        angle = ((part * bins_here + bins)[None, :] * time % samples) * (2.0 * math.pi / samples)
        tables.append(np.where(imaginary[None, :] == 1, -np.sin(angle), np.cos(angle)))
    exact = np.stack(tables)
    upper = exact.astype(jnp.bfloat16)
    lower = (exact - upper.astype(np.float64)).astype(jnp.bfloat16)
    return np.stack([upper, lower], axis=1)


def spread_tables(parts_of, terms, group):
    depth = group * parts_of
    column = np.arange(depth)
    spread = (np.arange(parts_of)[:, None] == column[None, :] % parts_of).astype(jnp.bfloat16)
    quarter = np.arange(parts_of // terms * group)
    own_point = quarter[:, None] % group == column[None, :] // parts_of
    own_term = quarter[:, None] // group == (column[None, :] % parts_of) // terms
    return spread, (own_point & own_term).astype(jnp.bfloat16)


def wide_dot(rows, upper, lower, dims):
    head = rows.astype(jnp.bfloat16)
    tail = (rows - head.astype(jnp.float32)).astype(jnp.bfloat16)
    dot = functools.partial(
        lax.dot_general, dimension_numbers=(dims, ((), ())), preferred_element_type=jnp.float32
    )
    return dot(head, upper) + (dot(head, lower) + dot(tail, upper))


def hail(peers):
    barrier = pltpu.get_barrier_semaphore()
    for peer in peers:
        pl.semaphore_signal(barrier, inc=1, device_id=peer, device_id_type=MESH)


def await_all(peers):
    pl.semaphore_wait(pltpu.get_barrier_semaphore(), len(peers))


def greet(peers):
    hail(peers)
    await_all(peers)


def others(me, count):
    sense = jnp.where(2 * me < count, count - 1, 1)
    return [lax.rem(me + sense * step, count) for step in range(1, count)]


def gather_kernel(
    count,
    row_hbm,
    blocks_hbm,
    covered_hbm,
    crossover_hbm,
    strain_ref,
    scale_hbm,
    mechanism_hbm,
    slip_hbm,
    onset_hbm,
    band_hbm,
    table_hbm,
    spread_hbm,
    own_hbm,
    weights_ref,
    slots_ref,
    band_both,
    table_ref,
    weight_ref,
    spectrum_ref,
    row_ref,
    blocks_ref,
    covered_ref,
    crossover_ref,
    spread_ref,
    own_ref,
    scale_ref,
    mechanism_ref,
    slip_ref,
    onset_ref,
    band_ref,
    strain_buf,
    coded_ref,
    slot_pack,
    local_sem,
    load_sem,
    strain_sem,
    send_sem,
    recv_sem,
):
    me = lax.axis_index("pt")
    part = lax.axis_index("cmp")
    partner = {"cmp": 1 - part}
    blocks_here = scale_ref.shape[0]
    parts_of = scale_ref.shape[1]
    stretch = strain_ref.shape[0] // blocks_here
    block = stretch // parts_of
    bins = strain_ref.shape[1]
    half = bins // 2
    own = band_ref.shape[3]
    variations = band_ref.shape[1]
    samples = own * table_ref.shape[0]
    peers = others(me, count)
    friends = [{"pt": peer} for peer in peers] + [partner]
    hail(friends)
    loads = []
    for k, (source, target) in enumerate(
        (
            (row_hbm, row_ref),
            (blocks_hbm, blocks_ref),
            (covered_hbm, covered_ref),
            (slip_hbm, slip_ref),
            (onset_hbm, onset_ref),
            (band_hbm, band_ref),
            (mechanism_hbm, mechanism_ref),
            (scale_hbm, scale_ref),
            (spread_hbm, spread_ref),
            (own_hbm, own_ref),
            (crossover_hbm, crossover_ref),
        )
    ):
        copy = pltpu.make_async_copy(source, target, load_sem.at[k])
        copy.start()
        loads.append(copy)
    def strain_rows(b):
        return strain_ref.at[pl.ds(pl.multiple_of(b * stretch, stretch), stretch)]

    for b in range(blocks_here):
        pltpu.make_async_copy(strain_rows(b), strain_buf.at[pl.ds(b * stretch, stretch)], strain_sem.at[b]).start()
    table_copy = pltpu.make_async_copy(table_hbm, table_ref, local_sem)
    table_copy.start()
    for copy in loads[:5]:
        copy.wait()
    rupture = row_ref[me]
    covered = covered_ref[rupture]
    spread = variations // 2

    slot_total = blocks_ref.shape[1]

    def chosen(target):
        lowest = target * blocks_here
        slots = [jnp.int32(0)] * blocks_here
        found = jnp.int32(0)
        for slot in range(slot_total):
            named = blocks_ref[rupture, slot]
            live = (slot < covered) & (named >= lowest) & (named < lowest + blocks_here)
            for k in range(min(blocks_here, slot + 1)):
                slots[k] = jnp.where(live & (found == k), slot, slots[k])
            found = found + live.astype(jnp.int32)
        return slots

    for slot in range(slot_total):
        lanes = pl.ds(slot * block, block)
        onset = (onset_ref[0, :, lanes] - onset_middle) * onset_steps
        onset = jnp.minimum(jnp.round(onset), onset_middle * onset_steps - 1.0)
        slip = slip_ref[0, :, lanes].astype(jnp.float32) * slip_steps
        for h in range(2):
            lines = slice(h * spread, (h + 1) * spread)
            coded_ref[slot, h] = (
                jnp.concatenate([onset[lines], slip[lines]], axis=0)
                .astype(jnp.int32)
                .astype(coded_ref.dtype)
            )

    def pack(step, carry):
        for k, slot in enumerate(chosen(others(me, count)[step])):
            slot_pack[step, k] = coded_ref[slot]

    for step in range(count - 1):
        pack(step, 0)
    await_all(friends)
    sends = []
    for step, peer in enumerate(peers):
        copy = pltpu.make_async_remote_copy(
            src_ref=slot_pack.at[step],
            dst_ref=slots_ref.at[me],
            send_sem=send_sem.at[step],
            recv_sem=recv_sem.at[me],
            device_id={"pt": peer},
            device_id_type=MESH,
        )
        copy.start()
        sends.append(copy)
    loads[5].wait()
    for c in range(2):
        band_both[0, pl.ds(c * variations, variations), :] = band_ref[0, :, c, :]
    band_copy = pltpu.make_async_remote_copy(
        src_ref=band_both.at[0],
        dst_ref=band_both.at[1],
        send_sem=send_sem.at[count - 1],
        recv_sem=recv_sem.at[count],
        device_id=partner,
        device_id_type=MESH,
    )
    band_copy.start()
    for k, slot in enumerate(chosen(me)):
        slots_ref[me, k] = coded_ref[slot]

    for copy in loads[6:]:
        copy.wait()
    crossing = crossover_ref[rupture].astype(jnp.float32)
    column = lax.broadcasted_iota(jnp.int32, weight_ref.shape[1:], 1)
    for q in range(weight_ref.shape[0]):
        frequency_id = q * bins + (column // bins) * half + column % half
        frequency = frequency_id.astype(jnp.float32)
        taper = jnp.clip((crossing - frequency) / taper_width + 0.5, 0.0, 1.0)
        weight_ref[q] = taper * jnp.where(frequency_id == 0, 1.0, 2.0) / samples
    group = 8
    pair = 2 * group
    depth = group * parts_of
    low_lanes = lax.broadcasted_iota(jnp.int32, (pair, bins), 1) < half
    dot = functools.partial(jnp.dot, preferred_element_type=jnp.float32)

    def make_block(b, carry):
        pltpu.make_async_copy(strain_rows(b), strain_buf.at[pl.ds(b * stretch, stretch)], strain_sem.at[b]).wait()
        moment = mechanism_ref[:, pl.ds(pl.multiple_of(b * block, block), block)]
        factors = jnp.transpose(jnp.concatenate([moment] * 4, axis=0)) * scale_ref[pl.ds(b, 1), :]
        head = factors.astype(jnp.bfloat16)
        tail = (factors - head.astype(jnp.float32)).astype(jnp.bfloat16)
        wide = [dot(piece, spread_ref[...]) for piece in (head, tail)]
        for first in range(0, block, pair):
            sums = []
            for start in (first, first + group):
                rows = []
                for piece in wide:
                    tile = piece[start : start + group]
                    twice = jnp.concatenate([tile, tile], axis=0).astype(jnp.bfloat16)
                    rows += [twice * own_ref[:pair], twice * own_ref[pair:]]
                product = dot(
                    jnp.concatenate(rows, axis=0),
                    strain_buf[pl.ds(pl.multiple_of(b * stretch + start * parts_of, depth), depth), :],
                )
                sums.append(product[: 2 * pair] + product[2 * pair :])
            quarters = [
                jnp.concatenate([part_sum[q * group : (q + 1) * group] for part_sum in sums], axis=0)
                for q in range(4)
            ]
            for c in range(2):
                real, imag = quarters[c], quarters[2 + c]
                real_turned = pltpu.roll(real, half, 1)
                imag_turned = pltpu.roll(imag, half, 1)
                lanes = pl.ds(c * bins, bins)
                pieces = (
                    (0, 0, real, imag_turned),
                    (0, 1, imag, -real_turned),
                    (1, 0, real_turned, imag),
                    (1, 1, imag_turned, -real),
                )
                for which, lower, first_half, second_half in pieces:
                    weights_ref[b, which, pl.ds(lower * block + first, pair), lanes] = jnp.where(
                        low_lanes, first_half, second_half
                    ).astype(jnp.bfloat16)
        return carry

    lax.fori_loop(0, blocks_here, make_block, 0)

    table_copy.wait()
    band_copy.wait()
    down = ((1,), (0,))
    lines = [pl.ds(pl.multiple_of(lax.rem(part + k, 2) * own, own), own) for k in range(2)]
    bands = [
        wide_dot(band_both[0], table_ref[q, 0, lines[0], :], table_ref[q, 1, lines[0], :], down)
        + wide_dot(band_both[1], table_ref[q, 0, lines[1], :], table_ref[q, 1, lines[1], :], down)
        for q in range(spectrum_ref.shape[0])
    ]
    for q, band in enumerate(bands):
        spectrum_ref[q] = band
    for copy in sends:
        copy.wait_send()
    for peer in peers:
        arrival = slots_ref.at[peer]
        pltpu.make_async_remote_copy(
            src_ref=arrival,
            dst_ref=arrival,
            send_sem=send_sem.at[0],
            recv_sem=recv_sem.at[peer],
            device_id={"pt": peer},
            device_id_type=MESH,
        ).wait_recv()


def turn(first, second):
    return (
        first[0] * second[0] - first[1] * second[1],
        first[0] * second[1] + first[1] * second[0],
    )


def quarter_unit(angle):
    off = angle - 0.25 * math.pi
    square = off * off
    sine = off * (
        1.0
        + square * (-1.0 / 6 + square * (1.0 / 120 + square * (-1.0 / 5040 + square * (1.0 / 362880))))
    )
    cosine = 1.0 + square * (
        -0.5
        + square
        * (1.0 / 24 + square * (-1.0 / 720 + square * (1.0 / 40320 + square * (-1.0 / 3628800))))
    )
    scale = math.sqrt(0.5)
    return scale * (cosine - sine), scale * (cosine + sine)


def slot_rows(slots_ref, row, found, spread):
    pieces = [
        slots_ref[row, found, h].astype(jnp.int32).astype(jnp.float32)
        for h in range(slots_ref.shape[2])
    ]
    onset = jnp.concatenate([piece[:spread] for piece in pieces], axis=0)
    slip = jnp.concatenate([piece[spread:] for piece in pieces], axis=0)
    return onset / onset_steps + onset_middle, slip / slip_steps


def with_sums(action):
    units = [pltpu.ACC(unit)((256, 256), jnp.float32) for unit in (0, 0, 1, 1)]
    pl.run_scoped(lambda *sums: action((sums[:2], sums[2:])), *units)


def pair_spectrum(step_angle, slots_ref, weights_ref, sums, row, found, local):
    halves, depth, columns = weights_ref.shape[1:]
    spread = slots_ref.shape[3] // 2
    bins = columns // 2
    half = bins // 2
    fine_total = 16
    reach = fine_total // 2
    onset, slip = slot_rows(slots_ref, row, found, spread)
    variations = onset.shape[0]
    powers = [None, quarter_unit(step_angle * onset)]
    for k in range(2, reach + 1):
        powers.append(turn(powers[k // 2], powers[k - k // 2]))
    leap = turn(powers[reach], powers[reach])
    far = leap
    for unused in range(int(math.log2(bins // fine_total))):
        far = turn(far, far)
    second_part = lax.axis_index("cmp") == 1
    centre = turn(
        powers[reach],
        (slip * jnp.where(second_part, far[0], 1.0), slip * jnp.where(second_part, far[1], 0.0)),
    )
    rounds = half // fine_total
    centres = [centre]
    for unused in range(halves * rounds - 1):
        centres.append(turn(centres[-1], leap))
    for which in range(halves):
        pltpu.matmul_push_rhs(weights_ref[local, which], 0, which)
    lane_bin = lax.broadcasted_iota(jnp.int32, (8, 128), 1) % half
    tiles = [
        [
            [jnp.zeros((8, 128), jnp.float32) for lane in range(columns // 128)]
            for line in range(variations // 8)
        ]
        for which in range(halves)
    ]

    def start(which, h):
        middle = centres[which * rounds + h]
        near = [None] * fine_total
        near[reach] = middle
        for k in range(1, reach + 1):
            cos_cos, sin_sin = middle[0] * powers[k][0], middle[1] * powers[k][1]
            sin_cos, cos_sin = middle[1] * powers[k][0], middle[0] * powers[k][1]
            near[reach - k] = (cos_cos + sin_sin, sin_cos - cos_sin)
            if k < reach:
                near[reach + k] = (cos_cos - sin_sin, sin_cos + cos_sin)
        pieces = [
            jnp.concatenate([phase[0].astype(jnp.bfloat16), phase[1].astype(jnp.bfloat16)], axis=1)
            for phase in near
        ]
        pltpu.matmul_acc_lhs(
            sums[which][h % 2], jnp.concatenate(pieces, axis=0), load_staged_rhs=0 if h == 0 else None
        )

    def finish(which, h):
        product = pltpu.matmul_pop(sums[which][h % 2])
        for k in range(fine_total):
            here = lane_bin == h * fine_total + k
            for line, across in enumerate(tiles[which]):
                first = k * variations + 8 * line
                for lane in range(len(across)):
                    across[lane] = jnp.where(
                        here, product[first : first + 8, 128 * lane : 128 * (lane + 1)], across[lane]
                    )

    for h in range(rounds + 1):
        for which in range(halves):
            if h < rounds:
                start(which, h)
            if h > 0:
                finish(which, h - 1)
    return [
        jnp.concatenate([jnp.concatenate(across, axis=1) for across in lines], axis=0)
        for lines in tiles
    ]


def pair_kernel(
    step_angle,
    row_ref,
    blocks_ref,
    covered_ref,
    weights_ref,
    slots_ref,
    total_ref,
    codes_ref,
):
    me = lax.axis_index("pt")
    blocks_here = weights_ref.shape[0]
    rows = slots_ref.shape[0]
    later = codes_ref.shape[0]
    lowest = me * blocks_here
    total_ref[...] = jnp.zeros_like(total_ref)
    codes_ref[...] = jnp.full(codes_ref.shape, -1, jnp.int32)

    def one_row(row, seen):
        rupture = row_ref[row]

        def one_slot(slot, carry):
            found, seen = carry
            local = blocks_ref[rupture, slot] - lowest
            live = (local >= 0) & (local < blocks_here)

            @pl.when(live & (seen < later))
            def _():
                code = (row * blocks_here + local) * blocks_here + found
                codes_ref[pl.ds(seen, 1)] = jnp.full((1,) + codes_ref.shape[1:], code, jnp.int32)

            def add(sums):
                spectra = pair_spectrum(
                    step_angle, slots_ref, weights_ref, sums, row, found, local
                )
                for which, spectrum in enumerate(spectra):
                    total_ref[row, which] += spectrum

            @pl.when(live & (seen >= later))
            def _():
                with_sums(add)

            return found + live.astype(jnp.int32), seen + live.astype(jnp.int32)

        return lax.fori_loop(0, covered_ref[rupture], one_slot, (jnp.int32(0), seen))[1]

    lax.fori_loop(0, rows, one_row, jnp.int32(0))


def merge_kernel(
    count,
    step_angle,
    begun_ref,
    codes_ref,
    slots_ref,
    weights_ref,
    weight_ref,
    spectrum_ref,
    excess_ref,
    total_ref,
    partial_ref,
    arrived,
    send_sem,
    recv_sem,
):
    me = lax.axis_index("pt")
    part = lax.axis_index("cmp")
    blocks_here = weights_ref.shape[0]
    rows, halves, variations, columns = begun_ref.shape
    parts = weight_ref.shape[0]
    bins = columns // 2
    friends = [{"pt": me, "cmp": 1 - part}]
    for peer in others(me, count):
        friends += [{"pt": peer, "cmp": part}, {"pt": peer, "cmp": 1 - part}]
    hail(friends)
    total_ref[...] = begun_ref[...]

    def first_pairs(sums):
        for j in range(codes_ref.shape[0]):
            code = codes_ref[j, 0, 0]
            safe = jnp.maximum(code, 0)
            holder = lax.div(safe, blocks_here)
            row = lax.div(holder, blocks_here)
            spectra = pair_spectrum(
                step_angle,
                slots_ref,
                weights_ref,
                sums,
                row,
                safe - holder * blocks_here,
                holder - row * blocks_here,
            )
            chosen = jnp.where(code < 0, -1, row)
            for other in range(rows):
                share = jnp.where(chosen == other, 1.0, 0.0)
                for which in range(halves):
                    total_ref[other, which] += share * spectra[which]

    with_sums(first_pairs)
    partial_ref[...] = total_ref[...].astype(partial_ref.dtype)
    await_all(friends)
    sends = []
    for step, friend in enumerate(friends):
        copy = pltpu.make_async_remote_copy(
            src_ref=partial_ref.at[friend["pt"]],
            dst_ref=arrived.at[me, part],
            send_sem=send_sem.at[step],
            recv_sem=recv_sem.at[me, part],
            device_id=friend,
            device_id_type=MESH,
        )
        copy.start()
        sends.append(copy)
    arrived[me, part] = partial_ref[me]
    for friend in friends:
        arrival = arrived.at[friend["pt"], friend["cmp"]]
        pltpu.make_async_remote_copy(
            src_ref=arrival,
            dst_ref=arrival,
            send_sem=send_sem.at[0],
            recv_sem=recv_sem.at[friend["pt"], friend["cmp"]],
            device_id=friend,
            device_id_type=MESH,
        ).wait_recv()
    for q in range(parts):
        weight = weight_ref[q]
        total = arrived[0, q].astype(jnp.float32)
        for source in range(1, count):
            total = total + arrived[source, q].astype(jnp.float32)
        for c in range(2):
            here = pl.ds(c * variations, variations)
            lanes = slice(c * bins, (c + 1) * bins)
            whole = jnp.concatenate([total[which][:, lanes] for which in range(halves)], axis=1)
            excess_ref[q, here, :] = (whole - spectrum_ref[q, here, :]) * weight
    for copy in sends:
        copy.wait_send()


def final_kernel(excess_ref, band_ref, table_ref, out_ref):
    part = lax.axis_index("cmp")
    variations = out_ref.shape[1]
    own = out_ref.shape[3]
    across = ((1,), (1,))
    low = band_ref[0]
    steps = pl.ds(pl.multiple_of(part * own, own), own)
    for q in range(table_ref.shape[0]):
        low = low + wide_dot(excess_ref[q], table_ref[q, 0, steps, :], table_ref[q, 1, steps, :], across)
    for c in range(2):
        out_ref[0, :, c, :] = low[c * variations : (c + 1) * variations]


def stay(array):
    return pltpu.with_memory_space_constraint(array, VMEM)


def body(
    strain_green,
    green_scale,
    mechanism,
    slip_amplitude,
    onset_time,
    rupture_row,
    rupture_blocks,
    block_count,
    crossover,
    high_band,
):
    points, parts_of, bins = strain_green.shape
    blocks_here = green_scale.shape[0]
    block = points // blocks_here
    rows_here, variations, slots = slip_amplitude.shape
    count = lax.axis_size("pt")
    parts = lax.axis_size("cmp")
    own = high_band.shape[3]
    samples = own * parts
    rows = rows_here * count
    tables = jnp.asarray(basis_tables(bins, parts, samples))
    spread, own_terms = spread_tables(parts_of, mechanism.shape[0], 8)
    vmem = pl.BlockSpec(memory_space=VMEM)
    smem = pl.BlockSpec(memory_space=SMEM)
    anywhere = pl.BlockSpec(memory_space=pltpu.HBM)
    grant = 24 * 1024 * 1024
    later = 4
    step_angle = 2.0 * math.pi / samples
    share = (blocks_here, 2, variations, block)
    weights, slots_all, bands, table, weight, band_spectrum = pl.pallas_call(
        functools.partial(gather_kernel, count),
        out_shape=(
            VMEM((blocks_here, 2, 2 * block, 2 * bins), jnp.bfloat16),
            VMEM((rows,) + share, jnp.int16),
            VMEM((2, 2 * variations, own), jnp.float32),
            VMEM(tables.shape, jnp.bfloat16),
            VMEM((parts, variations, 2 * bins), jnp.float32),
            VMEM((parts, 2 * variations, 2 * bins), jnp.float32),
        ),
        in_specs=[anywhere] * 13,
        out_specs=(vmem,) * 6,
        scratch_shapes=[
            SMEM(rupture_row.shape, jnp.int32),
            SMEM(rupture_blocks.shape, jnp.int32),
            SMEM(block_count.shape, jnp.int32),
            SMEM(crossover.shape, jnp.int32),
            VMEM(spread.shape, jnp.bfloat16),
            VMEM(own_terms.shape, jnp.bfloat16),
            VMEM(green_scale.shape, green_scale.dtype),
            VMEM(mechanism.shape, mechanism.dtype),
            VMEM(slip_amplitude.shape, slip_amplitude.dtype),
            VMEM(onset_time.shape, onset_time.dtype),
            VMEM(high_band.shape, high_band.dtype),
            VMEM((points * parts_of, bins), strain_green.dtype),
            VMEM((slots // block, 2, variations, block), jnp.int16),
            VMEM((count - 1,) + share, jnp.int16),
            pltpu.SemaphoreType.DMA,
            pltpu.SemaphoreType.DMA((11,)),
            pltpu.SemaphoreType.DMA((blocks_here,)),
            pltpu.SemaphoreType.DMA((count,)),
            pltpu.SemaphoreType.DMA((count + 1,)),
        ],
        compiler_params=pltpu.CompilerParams(collective_id=0, has_side_effects=True),
        name="gather",
    )(
        rupture_row,
        rupture_blocks,
        block_count,
        crossover,
        strain_green.reshape(points * parts_of, bins),
        green_scale,
        mechanism,
        slip_amplitude,
        onset_time,
        high_band,
        tables,
        jnp.asarray(spread),
        jnp.asarray(own_terms),
    )
    begun, codes = pl.pallas_call(
        functools.partial(pair_kernel, step_angle),
        out_shape=(
            VMEM((rows, 2, variations, 2 * bins), jnp.float32),
            VMEM((later, 8, 128), jnp.int32),
        ),
        in_specs=[smem, smem, smem, vmem, vmem],
        out_specs=(vmem, vmem),
        compiler_params=pltpu.CompilerParams(vmem_limit_bytes=grant),
        name="pairs",
    )(rupture_row, rupture_blocks, block_count, stay(weights), stay(slots_all))
    excess = pl.pallas_call(
        functools.partial(merge_kernel, count, step_angle),
        out_shape=VMEM((2, 2 * variations, 2 * bins), jnp.float32),
        in_specs=[vmem] * 6,
        out_specs=vmem,
        scratch_shapes=[
            VMEM((rows, 2, variations, 2 * bins), jnp.float32),
            VMEM((rows, 2, variations, 2 * bins), jnp.bfloat16),
            VMEM((count, parts, 2, variations, 2 * bins), jnp.bfloat16),
            pltpu.SemaphoreType.DMA((2 * count - 1,)),
            pltpu.SemaphoreType.DMA((count, parts)),
        ],
        compiler_params=pltpu.CompilerParams(collective_id=1, has_side_effects=True, vmem_limit_bytes=grant),
        name="merge",
    )(stay(begun), stay(codes), stay(slots_all), stay(weights), stay(weight), stay(band_spectrum))
    return pl.pallas_call(
        final_kernel,
        out_shape=jax.ShapeDtypeStruct(high_band.shape, high_band.dtype),
        in_specs=[vmem, vmem, vmem],
        out_specs=vmem,
        compiler_params=pltpu.CompilerParams(vmem_limit_bytes=grant),
        name="final",
    )(stay(excess), stay(bands), stay(table))


def solution(mesh):
    return jax.shard_map(
        body,
        mesh=mesh,
        in_specs=(
            P(("site", "pt"), None, "cmp"),
            P(("site", "pt"), None),
            P(None, "pt"),
            P("pt", "var", None),
            P("pt", "var", None),
            P(),
            P(),
            P(),
            P(),
            P(("site", "pt"), "var", None, "cmp"),
        ),
        out_specs=P(("site", "pt"), "var", None, "cmp"),
        check_vma=False,
    )
```

```python
import functools
import math

import jax
import jax.numpy as jnp
import numpy as np
from jax import lax
from jax.experimental import pallas as pl
from jax.experimental.pallas import tpu as pltpu
from jax.sharding import PartitionSpec as P

taper_width = 8.0
onset_middle = 64.0
onset_steps = 512.0
slip_steps = 1024.0
MESH = pl.DeviceIdType.MESH
VMEM = pltpu.VMEM
SMEM = pltpu.SMEM


def column_bins(bins_here):
    half = bins_here // 2
    column = np.arange(2 * bins_here)
    return (column // bins_here) * half + column % half, (column // half) % 2


def basis_tables(bins_here, parts, samples):
    bins, imaginary = column_bins(bins_here)
    time = np.arange(samples)[:, None]
    tables = []
    for part in range(parts):
        angle = ((part * bins_here + bins)[None, :] * time % samples) * (2.0 * math.pi / samples)
        tables.append(np.where(imaginary[None, :] == 1, -np.sin(angle), np.cos(angle)))
    exact = np.stack(tables)
    upper = exact.astype(jnp.bfloat16)
    lower = (exact - upper.astype(np.float64)).astype(jnp.bfloat16)
    return np.stack([upper, lower], axis=1)


def spread_tables(parts_of, terms, group):
    depth = group * parts_of
    column = np.arange(depth)
    spread = (np.arange(parts_of)[:, None] == column[None, :] % parts_of).astype(jnp.bfloat16)
    quarter = np.arange(parts_of // terms * group)
    own_point = quarter[:, None] % group == column[None, :] // parts_of
    own_term = quarter[:, None] // group == (column[None, :] % parts_of) // terms
    return spread, (own_point & own_term).astype(jnp.bfloat16)


def wide_dot(rows, upper, lower, dims):
    head = rows.astype(jnp.bfloat16)
    tail = (rows - head.astype(jnp.float32)).astype(jnp.bfloat16)
    dot = functools.partial(
        lax.dot_general, dimension_numbers=(dims, ((), ())), preferred_element_type=jnp.float32
    )
    return dot(head, upper) + (dot(head, lower) + dot(tail, upper))


def hail(peers):
    barrier = pltpu.get_barrier_semaphore()
    for peer in peers:
        pl.semaphore_signal(barrier, inc=1, device_id=peer, device_id_type=MESH)


def await_all(peers):
    pl.semaphore_wait(pltpu.get_barrier_semaphore(), len(peers))


def greet(peers):
    hail(peers)
    await_all(peers)


def others(me, count):
    sense = jnp.where(2 * me < count, count - 1, 1)
    return [lax.rem(me + sense * step, count) for step in range(1, count)]


def gather_kernel(
    count,
    row_hbm,
    blocks_hbm,
    covered_hbm,
    crossover_hbm,
    strain_ref,
    scale_hbm,
    mechanism_hbm,
    slip_hbm,
    onset_hbm,
    band_hbm,
    table_hbm,
    spread_hbm,
    own_hbm,
    weights_ref,
    slots_ref,
    band_both,
    table_ref,
    weight_ref,
    spectrum_ref,
    codes_ref,
    row_ref,
    blocks_ref,
    covered_ref,
    crossover_ref,
    spread_ref,
    own_ref,
    scale_ref,
    mechanism_ref,
    slip_ref,
    onset_ref,
    band_ref,
    strain_buf,
    coded_ref,
    slot_pack,
    local_sem,
    load_sem,
    strain_sem,
    send_sem,
    recv_sem,
):
    me = lax.axis_index("pt")
    part = lax.axis_index("cmp")
    partner = {"cmp": 1 - part}
    blocks_here = scale_ref.shape[0]
    parts_of = scale_ref.shape[1]
    stretch = strain_ref.shape[0] // blocks_here
    block = stretch // parts_of
    bins = strain_ref.shape[1]
    half = bins // 2
    own = band_ref.shape[3]
    variations = band_ref.shape[1]
    samples = own * table_ref.shape[0]
    peers = others(me, count)
    friends = [{"pt": peer} for peer in peers] + [partner]
    hail(friends)
    loads = []
    for k, (source, target) in enumerate(
        (
            (row_hbm, row_ref),
            (blocks_hbm, blocks_ref),
            (covered_hbm, covered_ref),
            (slip_hbm, slip_ref),
            (onset_hbm, onset_ref),
            (band_hbm, band_ref),
            (mechanism_hbm, mechanism_ref),
            (scale_hbm, scale_ref),
            (spread_hbm, spread_ref),
            (own_hbm, own_ref),
            (crossover_hbm, crossover_ref),
        )
    ):
        copy = pltpu.make_async_copy(source, target, load_sem.at[k])
        copy.start()
        loads.append(copy)
    def strain_rows(b):
        return strain_ref.at[pl.ds(pl.multiple_of(b * stretch, stretch), stretch)]

    for b in range(blocks_here):
        pltpu.make_async_copy(strain_rows(b), strain_buf.at[pl.ds(b * stretch, stretch)], strain_sem.at[b]).start()
    table_copy = pltpu.make_async_copy(table_hbm, table_ref, local_sem)
    table_copy.start()
    for copy in loads[:3]:
        copy.wait()
    rupture = row_ref[me]
    covered = covered_ref[rupture]
    spread = variations // 2

    slot_total = blocks_ref.shape[1]

    def chosen(target):
        lowest = target * blocks_here
        slots = [jnp.int32(0)] * blocks_here
        found = jnp.int32(0)
        for slot in range(slot_total):
            named = blocks_ref[rupture, slot]
            live = (slot < covered) & (named >= lowest) & (named < lowest + blocks_here)
            for k in range(min(blocks_here, slot + 1)):
                slots[k] = jnp.where(live & (found == k), slot, slots[k])
            found = found + live.astype(jnp.int32)
        return slots

    sent = [chosen(peer) for peer in peers]
    kept = chosen(me)
    for copy in loads[3:5]:
        copy.wait()
    for slot in range(slot_total):
        lanes = pl.ds(slot * block, block)
        onset = (onset_ref[0, :, lanes] - onset_middle) * onset_steps
        onset = jnp.minimum(jnp.round(onset), onset_middle * onset_steps - 1.0)
        slip = slip_ref[0, :, lanes].astype(jnp.float32) * slip_steps
        for h in range(2):
            lines = slice(h * spread, (h + 1) * spread)
            coded_ref[slot, h] = (
                jnp.concatenate([onset[lines], slip[lines]], axis=0)
                .astype(jnp.int32)
                .astype(coded_ref.dtype)
            )

    for step, slots in enumerate(sent):
        for k, slot in enumerate(slots):
            slot_pack[step, k] = coded_ref[slot]
    await_all(friends)
    sends = []
    for step, peer in enumerate(peers):
        copy = pltpu.make_async_remote_copy(
            src_ref=slot_pack.at[step],
            dst_ref=slots_ref.at[me],
            send_sem=send_sem.at[step],
            recv_sem=recv_sem.at[me],
            device_id={"pt": peer},
            device_id_type=MESH,
        )
        copy.start()
        sends.append(copy)
    loads[5].wait()
    for c in range(2):
        band_both[0, pl.ds(c * variations, variations), :] = band_ref[0, :, c, :]
    band_copy = pltpu.make_async_remote_copy(
        src_ref=band_both.at[0],
        dst_ref=band_both.at[1],
        send_sem=send_sem.at[count - 1],
        recv_sem=recv_sem.at[count],
        device_id=partner,
        device_id_type=MESH,
    )
    band_copy.start()
    for k, slot in enumerate(kept):
        slots_ref[me, k] = coded_ref[slot]

    for copy in loads[6:]:
        copy.wait()
    crossing = crossover_ref[rupture].astype(jnp.float32)
    column = lax.broadcasted_iota(jnp.int32, weight_ref.shape[1:], 1)
    for q in range(weight_ref.shape[0]):
        frequency_id = q * bins + (column // bins) * half + column % half
        frequency = frequency_id.astype(jnp.float32)
        taper = jnp.clip((crossing - frequency) / taper_width + 0.5, 0.0, 1.0)
        weight_ref[q] = taper * jnp.where(frequency_id == 0, 1.0, 2.0) / samples
    group = 8
    pair = 2 * group
    depth = group * parts_of
    low_lanes = lax.broadcasted_iota(jnp.int32, (pair, bins), 1) < half
    dot = functools.partial(jnp.dot, preferred_element_type=jnp.float32)

    def make_block(b, carry):
        pltpu.make_async_copy(strain_rows(b), strain_buf.at[pl.ds(b * stretch, stretch)], strain_sem.at[b]).wait()
        moment = mechanism_ref[:, pl.ds(pl.multiple_of(b * block, block), block)]
        factors = jnp.transpose(jnp.concatenate([moment] * 4, axis=0)) * scale_ref[pl.ds(b, 1), :]
        head = factors.astype(jnp.bfloat16)
        tail = (factors - head.astype(jnp.float32)).astype(jnp.bfloat16)
        wide = [dot(piece, spread_ref[...]) for piece in (head, tail)]
        for first in range(0, block, pair):
            sums = []
            for start in (first, first + group):
                rows = []
                for piece in wide:
                    tile = piece[start : start + group]
                    twice = jnp.concatenate([tile, tile], axis=0).astype(jnp.bfloat16)
                    rows += [twice * own_ref[:pair], twice * own_ref[pair:]]
                product = dot(
                    jnp.concatenate(rows, axis=0),
                    strain_buf[pl.ds(pl.multiple_of(b * stretch + start * parts_of, depth), depth), :],
                )
                sums.append(product[: 2 * pair] + product[2 * pair :])
            quarters = [
                jnp.concatenate([part_sum[q * group : (q + 1) * group] for part_sum in sums], axis=0)
                for q in range(4)
            ]
            for c in range(2):
                real, imag = quarters[c], quarters[2 + c]
                real_turned = pltpu.roll(real, half, 1)
                imag_turned = pltpu.roll(imag, half, 1)
                lanes = pl.ds(c * bins, bins)
                pieces = (
                    (0, 0, real, imag_turned),
                    (0, 1, imag, -real_turned),
                    (1, 0, real_turned, imag),
                    (1, 1, imag_turned, -real),
                )
                for which, lower, first_half, second_half in pieces:
                    weights_ref[b, which, pl.ds(lower * block + first, pair), lanes] = jnp.where(
                        low_lanes, first_half, second_half
                    ).astype(jnp.bfloat16)
        return carry

    lax.fori_loop(0, blocks_here, make_block, 0)

    later = codes_ref.shape[0] - 1
    lowest = me * blocks_here

    def list_row(row, carry):
        seen, codes = carry[0], list(carry[1:])
        covered_here = covered_ref[row_ref[row]]
        found = jnp.int32(0)
        for slot in range(slot_total):
            local = blocks_ref[row_ref[row], slot] - lowest
            live = (slot < covered_here) & (local >= 0) & (local < blocks_here)
            code = (row * blocks_here + local) * blocks_here + found
            for j in range(later):
                codes[j] = jnp.where(live & (seen == j), code, codes[j])
            found = found + live.astype(jnp.int32)
            seen = seen + live.astype(jnp.int32)
        return (seen, *codes)

    seen, *codes = lax.fori_loop(
        0, slots_ref.shape[0], list_row, (jnp.int32(0),) + (jnp.int32(-1),) * later
    )
    for j, code in enumerate([seen] + codes):
        codes_ref[j] = jnp.full(codes_ref.shape[1:], code, jnp.int32)
    table_copy.wait()
    band_copy.wait()
    down = ((1,), (0,))
    lines = [pl.ds(pl.multiple_of(lax.rem(part + k, 2) * own, own), own) for k in range(2)]
    bands = [
        wide_dot(band_both[0], table_ref[q, 0, lines[0], :], table_ref[q, 1, lines[0], :], down)
        + wide_dot(band_both[1], table_ref[q, 0, lines[1], :], table_ref[q, 1, lines[1], :], down)
        for q in range(spectrum_ref.shape[0])
    ]
    for q, band in enumerate(bands):
        spectrum_ref[q] = band
    for copy in sends:
        copy.wait_send()
    for peer in peers:
        arrival = slots_ref.at[peer]
        pltpu.make_async_remote_copy(
            src_ref=arrival,
            dst_ref=arrival,
            send_sem=send_sem.at[0],
            recv_sem=recv_sem.at[peer],
            device_id={"pt": peer},
            device_id_type=MESH,
        ).wait_recv()


def turn(first, second):
    return (
        first[0] * second[0] - first[1] * second[1],
        first[0] * second[1] + first[1] * second[0],
    )


def quarter_unit(angle):
    off = angle - 0.25 * math.pi
    square = off * off
    sine = off * (
        1.0
        + square * (-1.0 / 6 + square * (1.0 / 120 + square * (-1.0 / 5040 + square * (1.0 / 362880))))
    )
    cosine = 1.0 + square * (
        -0.5
        + square
        * (1.0 / 24 + square * (-1.0 / 720 + square * (1.0 / 40320 + square * (-1.0 / 3628800))))
    )
    scale = math.sqrt(0.5)
    return scale * (cosine - sine), scale * (cosine + sine)


def slot_rows(slots_ref, row, found, spread):
    pieces = [
        slots_ref[row, found, h].astype(jnp.int32).astype(jnp.float32)
        for h in range(slots_ref.shape[2])
    ]
    onset = jnp.concatenate([piece[:spread] for piece in pieces], axis=0)
    slip = jnp.concatenate([piece[spread:] for piece in pieces], axis=0)
    return onset / onset_steps + onset_middle, slip / slip_steps


def with_sums(action):
    units = [pltpu.ACC(unit)((256, 256), jnp.float32) for unit in (0, 0, 1, 1)]
    pl.run_scoped(lambda *sums: action((sums[:2], sums[2:])), *units)


def pair_spectrum(step_angle, slots_ref, weights_ref, sums, row, found, local):
    halves, depth, columns = weights_ref.shape[1:]
    spread = slots_ref.shape[3] // 2
    bins = columns // 2
    half = bins // 2
    fine_total = 16
    reach = fine_total // 2
    onset, slip = slot_rows(slots_ref, row, found, spread)
    variations = onset.shape[0]
    powers = [None, quarter_unit(step_angle * onset)]
    for k in range(2, reach + 1):
        powers.append(turn(powers[k // 2], powers[k - k // 2]))
    leap = turn(powers[reach], powers[reach])
    far = leap
    for unused in range(int(math.log2(bins // fine_total))):
        far = turn(far, far)
    second_part = lax.axis_index("cmp") == 1
    centre = turn(
        powers[reach],
        (slip * jnp.where(second_part, far[0], 1.0), slip * jnp.where(second_part, far[1], 0.0)),
    )
    rounds = half // fine_total
    centres = [centre]
    for unused in range(halves * rounds - 1):
        centres.append(turn(centres[-1], leap))
    for which in range(halves):
        pltpu.matmul_push_rhs(weights_ref[local, which], 0, which)
    lane_bin = lax.broadcasted_iota(jnp.int32, (8, 128), 1) % half
    tiles = [
        [
            [jnp.zeros((8, 128), jnp.float32) for lane in range(columns // 128)]
            for line in range(variations // 8)
        ]
        for which in range(halves)
    ]

    def start(which, h):
        middle = centres[which * rounds + h]
        near = [None] * fine_total
        near[reach] = middle
        for k in range(1, reach + 1):
            cos_cos, sin_sin = middle[0] * powers[k][0], middle[1] * powers[k][1]
            sin_cos, cos_sin = middle[1] * powers[k][0], middle[0] * powers[k][1]
            near[reach - k] = (cos_cos + sin_sin, sin_cos - cos_sin)
            if k < reach:
                near[reach + k] = (cos_cos - sin_sin, sin_cos + cos_sin)
        pieces = [
            jnp.concatenate([phase[0].astype(jnp.bfloat16), phase[1].astype(jnp.bfloat16)], axis=1)
            for phase in near
        ]
        pltpu.matmul_acc_lhs(
            sums[which][h % 2], jnp.concatenate(pieces, axis=0), load_staged_rhs=0 if h == 0 else None
        )

    def finish(which, h):
        product = pltpu.matmul_pop(sums[which][h % 2])
        for k in range(fine_total):
            here = lane_bin == h * fine_total + k
            for line, across in enumerate(tiles[which]):
                first = k * variations + 8 * line
                for lane in range(len(across)):
                    across[lane] = jnp.where(
                        here, product[first : first + 8, 128 * lane : 128 * (lane + 1)], across[lane]
                    )

    for h in range(rounds + 1):
        for which in range(halves):
            if h < rounds:
                start(which, h)
            if h > 0:
                finish(which, h - 1)
    return [
        jnp.concatenate([jnp.concatenate(across, axis=1) for across in lines], axis=0)
        for lines in tiles
    ]


def pair_kernel(
    step_angle,
    row_hbm,
    blocks_hbm,
    covered_hbm,
    weights_ref,
    slots_ref,
    codes_ref,
    total_ref,
    row_ref,
    blocks_ref,
    covered_ref,
    load_sem,
):
    me = lax.axis_index("pt")
    blocks_here = weights_ref.shape[0]
    rows = slots_ref.shape[0]
    later = codes_ref.shape[0] - 1
    lowest = me * blocks_here

    @pl.when(codes_ref[0, 0, 0] > later)
    def _():
        loads = [
            pltpu.make_async_copy(source, target, load_sem.at[k])
            for k, (source, target) in enumerate(
                ((row_hbm, row_ref), (blocks_hbm, blocks_ref), (covered_hbm, covered_ref))
            )
        ]
        for copy in loads:
            copy.start()
        total_ref[...] = jnp.zeros_like(total_ref)
        for copy in loads:
            copy.wait()

        def one_row(row, seen):
            rupture = row_ref[row]

            def one_slot(slot, carry):
                found, seen = carry
                local = blocks_ref[rupture, slot] - lowest
                live = (local >= 0) & (local < blocks_here)

                def add(sums):
                    spectra = pair_spectrum(
                        step_angle, slots_ref, weights_ref, sums, row, found, local
                    )
                    for which, spectrum in enumerate(spectra):
                        total_ref[row, which] += spectrum

                @pl.when(live & (seen >= later))
                def _():
                    with_sums(add)

                return found + live.astype(jnp.int32), seen + live.astype(jnp.int32)

            return lax.fori_loop(0, covered_ref[rupture], one_slot, (jnp.int32(0), seen))[1]

        lax.fori_loop(0, rows, one_row, jnp.int32(0))


def merge_kernel(
    count,
    step_angle,
    begun_ref,
    codes_ref,
    slots_ref,
    weights_ref,
    weight_ref,
    spectrum_ref,
    excess_ref,
    total_ref,
    partial_ref,
    arrived,
    send_sem,
    recv_sem,
):
    me = lax.axis_index("pt")
    part = lax.axis_index("cmp")
    blocks_here = weights_ref.shape[0]
    rows, halves, variations, columns = begun_ref.shape
    parts = weight_ref.shape[0]
    bins = columns // 2
    friends = []
    for peer in others(me, count):
        friends += [{"pt": peer, "cmp": 0}, {"pt": peer, "cmp": 1}]
    friends.append({"pt": me, "cmp": 1 - part})
    hail(friends)
    later = codes_ref.shape[0] - 1
    begun = codes_ref[0, 0, 0] > later
    total_ref[...] = jnp.where(begun, begun_ref[...], 0.0)

    def first_pairs(sums):
        for j in range(later):
            code = codes_ref[j + 1, 0, 0]
            safe = jnp.maximum(code, 0)
            holder = lax.div(safe, blocks_here)
            row = lax.div(holder, blocks_here)
            spectra = pair_spectrum(
                step_angle,
                slots_ref,
                weights_ref,
                sums,
                row,
                safe - holder * blocks_here,
                holder - row * blocks_here,
            )
            chosen = jnp.where(code < 0, -1, row)
            for other in range(rows):
                share = jnp.where(chosen == other, 1.0, 0.0)
                for which in range(halves):
                    total_ref[other, which] += share * spectra[which]

    with_sums(first_pairs)
    partial_ref[...] = total_ref[...].astype(partial_ref.dtype)
    await_all(friends)
    sends = []
    for step, friend in enumerate(friends):
        copy = pltpu.make_async_remote_copy(
            src_ref=partial_ref.at[friend["pt"]],
            dst_ref=arrived.at[me, part],
            send_sem=send_sem.at[step],
            recv_sem=recv_sem.at[me, part],
            device_id=friend,
            device_id_type=MESH,
        )
        copy.start()
        sends.append(copy)
    arrived[me, part] = partial_ref[me]
    for friend in friends:
        arrival = arrived.at[friend["pt"], friend["cmp"]]
        pltpu.make_async_remote_copy(
            src_ref=arrival,
            dst_ref=arrival,
            send_sem=send_sem.at[0],
            recv_sem=recv_sem.at[friend["pt"], friend["cmp"]],
            device_id=friend,
            device_id_type=MESH,
        ).wait_recv()
    for q in range(parts):
        weight = weight_ref[q]
        total = arrived[0, q].astype(jnp.float32)
        for source in range(1, count):
            total = total + arrived[source, q].astype(jnp.float32)
        for c in range(2):
            here = pl.ds(c * variations, variations)
            lanes = slice(c * bins, (c + 1) * bins)
            whole = jnp.concatenate([total[which][:, lanes] for which in range(halves)], axis=1)
            excess_ref[q, here, :] = (whole - spectrum_ref[q, here, :]) * weight
    for copy in sends:
        copy.wait_send()


def final_kernel(excess_ref, band_ref, table_ref, out_ref):
    part = lax.axis_index("cmp")
    variations = out_ref.shape[1]
    own = out_ref.shape[3]
    across = ((1,), (1,))
    low = band_ref[0]
    steps = pl.ds(pl.multiple_of(part * own, own), own)
    for q in range(table_ref.shape[0]):
        low = low + wide_dot(excess_ref[q], table_ref[q, 0, steps, :], table_ref[q, 1, steps, :], across)
    for c in range(2):
        out_ref[0, :, c, :] = low[c * variations : (c + 1) * variations]


def stay(array):
    return pltpu.with_memory_space_constraint(array, VMEM)


def body(
    strain_green,
    green_scale,
    mechanism,
    slip_amplitude,
    onset_time,
    rupture_row,
    rupture_blocks,
    block_count,
    crossover,
    high_band,
):
    points, parts_of, bins = strain_green.shape
    blocks_here = green_scale.shape[0]
    block = points // blocks_here
    rows_here, variations, slots = slip_amplitude.shape
    count = lax.axis_size("pt")
    parts = lax.axis_size("cmp")
    own = high_band.shape[3]
    samples = own * parts
    rows = rows_here * count
    tables = jnp.asarray(basis_tables(bins, parts, samples))
    spread, own_terms = spread_tables(parts_of, mechanism.shape[0], 8)
    vmem = pl.BlockSpec(memory_space=VMEM)
    smem = pl.BlockSpec(memory_space=SMEM)
    anywhere = pl.BlockSpec(memory_space=pltpu.HBM)
    grant = 24 * 1024 * 1024
    later = 5
    step_angle = 2.0 * math.pi / samples
    share = (blocks_here, 2, variations, block)
    weights, slots_all, bands, table, weight, band_spectrum, codes = pl.pallas_call(
        functools.partial(gather_kernel, count),
        out_shape=(
            VMEM((blocks_here, 2, 2 * block, 2 * bins), jnp.bfloat16),
            VMEM((rows,) + share, jnp.int16),
            VMEM((2, 2 * variations, own), jnp.float32),
            VMEM(tables.shape, jnp.bfloat16),
            VMEM((parts, variations, 2 * bins), jnp.float32),
            VMEM((parts, 2 * variations, 2 * bins), jnp.float32),
            VMEM((later + 1, 8, 128), jnp.int32),
        ),
        in_specs=[anywhere] * 13,
        out_specs=(vmem,) * 7,
        scratch_shapes=[
            SMEM(rupture_row.shape, jnp.int32),
            SMEM(rupture_blocks.shape, jnp.int32),
            SMEM(block_count.shape, jnp.int32),
            SMEM(crossover.shape, jnp.int32),
            VMEM(spread.shape, jnp.bfloat16),
            VMEM(own_terms.shape, jnp.bfloat16),
            VMEM(green_scale.shape, green_scale.dtype),
            VMEM(mechanism.shape, mechanism.dtype),
            VMEM(slip_amplitude.shape, slip_amplitude.dtype),
            VMEM(onset_time.shape, onset_time.dtype),
            VMEM(high_band.shape, high_band.dtype),
            VMEM((points * parts_of, bins), strain_green.dtype),
            VMEM((slots // block, 2, variations, block), jnp.int16),
            VMEM((count - 1,) + share, jnp.int16),
            pltpu.SemaphoreType.DMA,
            pltpu.SemaphoreType.DMA((11,)),
            pltpu.SemaphoreType.DMA((blocks_here,)),
            pltpu.SemaphoreType.DMA((count,)),
            pltpu.SemaphoreType.DMA((count + 1,)),
        ],
        compiler_params=pltpu.CompilerParams(collective_id=0, has_side_effects=True),
        name="gather",
    )(
        rupture_row,
        rupture_blocks,
        block_count,
        crossover,
        strain_green.reshape(points * parts_of, bins),
        green_scale,
        mechanism,
        slip_amplitude,
        onset_time,
        high_band,
        tables,
        jnp.asarray(spread),
        jnp.asarray(own_terms),
    )
    begun = pl.pallas_call(
        functools.partial(pair_kernel, step_angle),
        out_shape=VMEM((rows, 2, variations, 2 * bins), jnp.float32),
        in_specs=[anywhere] * 3 + [vmem] * 3,
        out_specs=vmem,
        scratch_shapes=[
            SMEM(rupture_row.shape, jnp.int32),
            SMEM(rupture_blocks.shape, jnp.int32),
            SMEM(block_count.shape, jnp.int32),
            pltpu.SemaphoreType.DMA((3,)),
        ],
        compiler_params=pltpu.CompilerParams(vmem_limit_bytes=grant),
        name="pairs",
    )(rupture_row, rupture_blocks, block_count, stay(weights), stay(slots_all), stay(codes))
    excess = pl.pallas_call(
        functools.partial(merge_kernel, count, step_angle),
        out_shape=VMEM((2, 2 * variations, 2 * bins), jnp.float32),
        in_specs=[vmem] * 6,
        out_specs=vmem,
        scratch_shapes=[
            VMEM((rows, 2, variations, 2 * bins), jnp.float32),
            VMEM((rows, 2, variations, 2 * bins), jnp.bfloat16),
            VMEM((count, parts, 2, variations, 2 * bins), jnp.bfloat16),
            pltpu.SemaphoreType.DMA((2 * count - 1,)),
            pltpu.SemaphoreType.DMA((count, parts)),
        ],
        compiler_params=pltpu.CompilerParams(collective_id=1, has_side_effects=True, vmem_limit_bytes=grant),
        name="merge",
    )(stay(begun), stay(codes), stay(slots_all), stay(weights), stay(weight), stay(band_spectrum))
    return pl.pallas_call(
        final_kernel,
        out_shape=jax.ShapeDtypeStruct(high_band.shape, high_band.dtype),
        in_specs=[vmem, vmem, vmem],
        out_specs=vmem,
        compiler_params=pltpu.CompilerParams(vmem_limit_bytes=grant),
        name="final",
    )(stay(excess), stay(bands), stay(table))


def solution(mesh):
    return jax.shard_map(
        body,
        mesh=mesh,
        in_specs=(
            P(("site", "pt"), None, "cmp"),
            P(("site", "pt"), None),
            P(None, "pt"),
            P("pt", "var", None),
            P("pt", "var", None),
            P(),
            P(),
            P(),
            P(),
            P(("site", "pt"), "var", None, "cmp"),
        ),
        out_specs=P(("site", "pt"), "var", None, "cmp"),
        check_vma=False,
    )
```

```python
import functools
import math

import jax
import jax.numpy as jnp
import numpy as np
from jax import lax
from jax.experimental import pallas as pl
from jax.experimental.pallas import tpu as pltpu
from jax.sharding import PartitionSpec as P

taper_width = 8.0
onset_middle = 64.0
onset_steps = 512.0
slip_steps = 1024.0
MESH = pl.DeviceIdType.MESH
VMEM = pltpu.VMEM
SMEM = pltpu.SMEM


def column_bins(bins_here):
    half = bins_here // 2
    column = np.arange(2 * bins_here)
    return (column // bins_here) * half + column % half, (column // half) % 2


def basis_tables(bins_here, parts, samples):
    bins, imaginary = column_bins(bins_here)
    time = np.arange(samples)[:, None]
    tables = []
    for part in range(parts):
        angle = ((part * bins_here + bins)[None, :] * time % samples) * (2.0 * math.pi / samples)
        tables.append(np.where(imaginary[None, :] == 1, -np.sin(angle), np.cos(angle)))
    exact = np.stack(tables)
    upper = exact.astype(jnp.bfloat16)
    lower = (exact - upper.astype(np.float64)).astype(jnp.bfloat16)
    return np.stack([upper, lower], axis=1)


def spread_tables(parts_of, terms, group):
    depth = group * parts_of
    column = np.arange(depth)
    spread = (np.arange(parts_of)[:, None] == column[None, :] % parts_of).astype(jnp.bfloat16)
    quarter = np.arange(parts_of // terms * group)
    own_point = quarter[:, None] % group == column[None, :] // parts_of
    own_term = quarter[:, None] // group == (column[None, :] % parts_of) // terms
    return spread, (own_point & own_term).astype(jnp.bfloat16)


def wide_dot(rows, upper, lower, dims):
    head = rows.astype(jnp.bfloat16)
    tail = (rows - head.astype(jnp.float32)).astype(jnp.bfloat16)
    dot = functools.partial(
        lax.dot_general, dimension_numbers=(dims, ((), ())), preferred_element_type=jnp.float32
    )
    return dot(head, upper) + (dot(head, lower) + dot(tail, upper))


def hail(peers):
    barrier = pltpu.get_barrier_semaphore()
    for peer in peers:
        pl.semaphore_signal(barrier, inc=1, device_id=peer, device_id_type=MESH)


def await_all(peers):
    pl.semaphore_wait(pltpu.get_barrier_semaphore(), len(peers))


def greet(peers):
    hail(peers)
    await_all(peers)


def others(me, count):
    sense = jnp.where(2 * me < count, count - 1, 1)
    return [lax.rem(me + sense * step, count) for step in range(1, count)]


def gather_kernel(
    count,
    row_hbm,
    blocks_hbm,
    covered_hbm,
    crossover_hbm,
    strain_ref,
    scale_hbm,
    mechanism_hbm,
    slip_hbm,
    onset_hbm,
    band_hbm,
    table_hbm,
    spread_hbm,
    own_hbm,
    weights_ref,
    slots_ref,
    band_both,
    table_ref,
    weight_ref,
    spectrum_ref,
    codes_ref,
    row_ref,
    blocks_ref,
    covered_ref,
    crossover_ref,
    spread_ref,
    own_ref,
    scale_ref,
    mechanism_ref,
    slip_ref,
    onset_ref,
    band_ref,
    strain_buf,
    coded_ref,
    slot_pack,
    local_sem,
    load_sem,
    strain_sem,
    send_sem,
    recv_sem,
):
    me = lax.axis_index("pt")
    part = lax.axis_index("cmp")
    partner = {"cmp": 1 - part}
    blocks_here = scale_ref.shape[0]
    parts_of = scale_ref.shape[1]
    stretch = strain_ref.shape[0] // blocks_here
    block = stretch // parts_of
    bins = strain_ref.shape[1]
    half = bins // 2
    own = band_ref.shape[3]
    variations = band_ref.shape[1]
    samples = own * table_ref.shape[0]
    peers = others(me, count)
    friends = [{"pt": peer} for peer in peers] + [partner]
    hail(friends)
    loads = []
    for k, (source, target) in enumerate(
        (
            (row_hbm, row_ref),
            (blocks_hbm, blocks_ref),
            (covered_hbm, covered_ref),
            (slip_hbm, slip_ref),
            (onset_hbm, onset_ref),
            (band_hbm, band_ref),
            (mechanism_hbm, mechanism_ref),
            (scale_hbm, scale_ref),
            (spread_hbm, spread_ref),
            (own_hbm, own_ref),
            (crossover_hbm, crossover_ref),
        )
    ):
        copy = pltpu.make_async_copy(source, target, load_sem.at[k])
        copy.start()
        loads.append(copy)
    def strain_rows(b):
        return strain_ref.at[pl.ds(pl.multiple_of(b * stretch, stretch), stretch)]

    for b in range(blocks_here):
        pltpu.make_async_copy(strain_rows(b), strain_buf.at[pl.ds(b * stretch, stretch)], strain_sem.at[b]).start()
    table_copy = pltpu.make_async_copy(table_hbm, table_ref, local_sem)
    table_copy.start()
    for copy in loads[:3]:
        copy.wait()
    rupture = row_ref[me]
    covered = covered_ref[rupture]
    spread = variations // 2

    slot_total = blocks_ref.shape[1]

    def chosen(target):
        lowest = target * blocks_here
        slots = [jnp.int32(0)] * blocks_here
        found = jnp.int32(0)
        for slot in range(slot_total):
            named = blocks_ref[rupture, slot]
            live = (slot < covered) & (named >= lowest) & (named < lowest + blocks_here)
            for k in range(min(blocks_here, slot + 1)):
                slots[k] = jnp.where(live & (found == k), slot, slots[k])
            found = found + live.astype(jnp.int32)
        return slots

    sent = [chosen(peer) for peer in peers]
    kept = chosen(me)
    for copy in loads[3:5]:
        copy.wait()
    for slot in range(slot_total):
        lanes = pl.ds(slot * block, block)
        onset = (onset_ref[0, :, lanes] - onset_middle) * onset_steps
        onset = jnp.minimum(jnp.round(onset), onset_middle * onset_steps - 1.0)
        slip = slip_ref[0, :, lanes].astype(jnp.float32) * slip_steps
        for h in range(2):
            lines = slice(h * spread, (h + 1) * spread)
            coded_ref[slot, h] = (
                jnp.concatenate([onset[lines], slip[lines]], axis=0)
                .astype(jnp.int32)
                .astype(coded_ref.dtype)
            )

    for step, slots in enumerate(sent):
        for k, slot in enumerate(slots):
            slot_pack[step, k] = coded_ref[slot]
    await_all(friends)
    sends = []
    for step, peer in enumerate(peers):
        copy = pltpu.make_async_remote_copy(
            src_ref=slot_pack.at[step],
            dst_ref=slots_ref.at[me],
            send_sem=send_sem.at[step],
            recv_sem=recv_sem.at[me],
            device_id={"pt": peer},
            device_id_type=MESH,
        )
        copy.start()
        sends.append(copy)
    loads[5].wait()
    for c in range(2):
        band_both[0, pl.ds(c * variations, variations), :] = band_ref[0, :, c, :]
    band_copy = pltpu.make_async_remote_copy(
        src_ref=band_both.at[0],
        dst_ref=band_both.at[1],
        send_sem=send_sem.at[count - 1],
        recv_sem=recv_sem.at[count],
        device_id=partner,
        device_id_type=MESH,
    )
    band_copy.start()
    for k, slot in enumerate(kept):
        slots_ref[me, k] = coded_ref[slot]

    for copy in loads[6:]:
        copy.wait()
    crossing = crossover_ref[rupture].astype(jnp.float32)
    column = lax.broadcasted_iota(jnp.int32, weight_ref.shape[1:], 1)
    for q in range(weight_ref.shape[0]):
        frequency_id = q * bins + (column // bins) * half + column % half
        frequency = frequency_id.astype(jnp.float32)
        taper = jnp.clip((crossing - frequency) / taper_width + 0.5, 0.0, 1.0)
        weight_ref[q] = taper * jnp.where(frequency_id == 0, 1.0, 2.0) / samples
    group = 8
    pair = 2 * group
    depth = group * parts_of
    low_lanes = lax.broadcasted_iota(jnp.int32, (pair, bins), 1) < half
    dot = functools.partial(jnp.dot, preferred_element_type=jnp.float32)

    def make_block(b, carry):
        pltpu.make_async_copy(strain_rows(b), strain_buf.at[pl.ds(b * stretch, stretch)], strain_sem.at[b]).wait()
        moment = mechanism_ref[:, pl.ds(pl.multiple_of(b * block, block), block)]
        factors = jnp.transpose(jnp.concatenate([moment] * 4, axis=0)) * scale_ref[pl.ds(b, 1), :]
        head = factors.astype(jnp.bfloat16)
        tail = (factors - head.astype(jnp.float32)).astype(jnp.bfloat16)
        wide = [dot(piece, spread_ref[...]) for piece in (head, tail)]
        for first in range(0, block, pair):
            sums = []
            for start in (first, first + group):
                rows = []
                for piece in wide:
                    tile = piece[start : start + group]
                    twice = jnp.concatenate([tile, tile], axis=0).astype(jnp.bfloat16)
                    rows += [twice * own_ref[:pair], twice * own_ref[pair:]]
                product = dot(
                    jnp.concatenate(rows, axis=0),
                    strain_buf[pl.ds(pl.multiple_of(b * stretch + start * parts_of, depth), depth), :],
                )
                sums.append(product[: 2 * pair] + product[2 * pair :])
            quarters = [
                jnp.concatenate([part_sum[q * group : (q + 1) * group] for part_sum in sums], axis=0)
                for q in range(4)
            ]
            for c in range(2):
                real, imag = quarters[c], quarters[2 + c]
                real_turned = pltpu.roll(real, half, 1)
                imag_turned = pltpu.roll(imag, half, 1)
                lanes = pl.ds(c * bins, bins)
                pieces = (
                    (0, 0, real, imag_turned),
                    (0, 1, imag, -real_turned),
                    (1, 0, real_turned, imag),
                    (1, 1, imag_turned, -real),
                )
                for which, lower, first_half, second_half in pieces:
                    weights_ref[b, which, pl.ds(lower * block + first, pair), lanes] = jnp.where(
                        low_lanes, first_half, second_half
                    ).astype(jnp.bfloat16)
        return carry

    lax.fori_loop(0, blocks_here, make_block, 0)

    later = codes_ref.shape[0] - 1
    lowest = me * blocks_here

    def list_row(row, carry):
        seen, codes = carry[0], list(carry[1:])
        covered_here = covered_ref[row_ref[row]]
        found = jnp.int32(0)
        for slot in range(slot_total):
            local = blocks_ref[row_ref[row], slot] - lowest
            live = (slot < covered_here) & (local >= 0) & (local < blocks_here)
            code = (row * blocks_here + local) * blocks_here + found
            for j in range(later):
                codes[j] = jnp.where(live & (seen == j), code, codes[j])
            found = found + live.astype(jnp.int32)
            seen = seen + live.astype(jnp.int32)
        return (seen, *codes)

    seen, *codes = lax.fori_loop(
        0, slots_ref.shape[0], list_row, (jnp.int32(0),) + (jnp.int32(-1),) * later
    )
    for j, code in enumerate([seen] + codes):
        codes_ref[j] = jnp.full(codes_ref.shape[1:], code, jnp.int32)
    table_copy.wait()
    band_copy.wait()
    down = ((1,), (0,))
    lines = [pl.ds(pl.multiple_of(lax.rem(part + k, 2) * own, own), own) for k in range(2)]
    bands = [
        wide_dot(band_both[0], table_ref[q, 0, lines[0], :], table_ref[q, 1, lines[0], :], down)
        + wide_dot(band_both[1], table_ref[q, 0, lines[1], :], table_ref[q, 1, lines[1], :], down)
        for q in range(spectrum_ref.shape[0])
    ]
    for q, band in enumerate(bands):
        spectrum_ref[q] = band
    for copy in sends:
        copy.wait_send()
    for peer in peers:
        arrival = slots_ref.at[peer]
        pltpu.make_async_remote_copy(
            src_ref=arrival,
            dst_ref=arrival,
            send_sem=send_sem.at[0],
            recv_sem=recv_sem.at[peer],
            device_id={"pt": peer},
            device_id_type=MESH,
        ).wait_recv()


def turn(first, second):
    return (
        first[0] * second[0] - first[1] * second[1],
        first[0] * second[1] + first[1] * second[0],
    )


def quarter_unit(angle):
    off = angle - 0.25 * math.pi
    square = off * off
    sine = off * (
        1.0
        + square * (-1.0 / 6 + square * (1.0 / 120 + square * (-1.0 / 5040 + square * (1.0 / 362880))))
    )
    cosine = 1.0 + square * (
        -0.5
        + square
        * (1.0 / 24 + square * (-1.0 / 720 + square * (1.0 / 40320 + square * (-1.0 / 3628800))))
    )
    scale = math.sqrt(0.5)
    return scale * (cosine - sine), scale * (cosine + sine)


def slot_rows(slots_ref, row, found, spread):
    pieces = [
        slots_ref[row, found, h].astype(jnp.int32).astype(jnp.float32)
        for h in range(slots_ref.shape[2])
    ]
    onset = jnp.concatenate([piece[:spread] for piece in pieces], axis=0)
    slip = jnp.concatenate([piece[spread:] for piece in pieces], axis=0)
    return onset / onset_steps + onset_middle, slip / slip_steps


def with_sums(action):
    units = [pltpu.ACC(unit)((256, 256), jnp.float32) for unit in (0, 0, 1, 1)]
    pl.run_scoped(lambda *sums: action((sums[:2], sums[2:])), *units)


def pair_spectrum(step_angle, slots_ref, weights_ref, sums, row, found, local):
    halves, depth, columns = weights_ref.shape[1:]
    spread = slots_ref.shape[3] // 2
    bins = columns // 2
    half = bins // 2
    fine_total = 16
    reach = fine_total // 2
    onset, slip = slot_rows(slots_ref, row, found, spread)
    variations = onset.shape[0]
    powers = [None, quarter_unit(step_angle * onset)]
    for k in range(2, reach + 1):
        powers.append(turn(powers[k // 2], powers[k - k // 2]))
    leap = turn(powers[reach], powers[reach])
    far = leap
    for unused in range(int(math.log2(bins // fine_total))):
        far = turn(far, far)
    second_part = lax.axis_index("cmp") == 1
    centre = turn(
        powers[reach],
        (slip * jnp.where(second_part, far[0], 1.0), slip * jnp.where(second_part, far[1], 0.0)),
    )
    rounds = half // fine_total
    centres = [centre]
    for unused in range(halves * rounds - 1):
        centres.append(turn(centres[-1], leap))
    for which in range(halves):
        pltpu.matmul_push_rhs(weights_ref[local, which], 0, which)
    lane_bin = lax.broadcasted_iota(jnp.int32, (8, 128), 1) % half
    tiles = [
        [
            [jnp.zeros((8, 128), jnp.float32) for lane in range(columns // 128)]
            for line in range(variations // 8)
        ]
        for which in range(halves)
    ]

    def start(which, h):
        middle = centres[which * rounds + h]
        near = [None] * fine_total
        near[reach] = middle
        for k in range(1, reach + 1):
            cos_cos, sin_sin = middle[0] * powers[k][0], middle[1] * powers[k][1]
            sin_cos, cos_sin = middle[1] * powers[k][0], middle[0] * powers[k][1]
            near[reach - k] = (cos_cos + sin_sin, sin_cos - cos_sin)
            if k < reach:
                near[reach + k] = (cos_cos - sin_sin, sin_cos + cos_sin)
        pieces = [
            jnp.concatenate([phase[0].astype(jnp.bfloat16), phase[1].astype(jnp.bfloat16)], axis=1)
            for phase in near
        ]
        pltpu.matmul_acc_lhs(
            sums[which][h % 2], jnp.concatenate(pieces, axis=0), load_staged_rhs=0 if h == 0 else None
        )

    def finish(which, h):
        product = pltpu.matmul_pop(sums[which][h % 2])
        for k in range(fine_total):
            here = lane_bin == h * fine_total + k
            for line, across in enumerate(tiles[which]):
                first = k * variations + 8 * line
                for lane in range(len(across)):
                    across[lane] = jnp.where(
                        here, product[first : first + 8, 128 * lane : 128 * (lane + 1)], across[lane]
                    )

    for h in range(rounds + 1):
        for which in range(halves):
            if h < rounds:
                start(which, h)
            if h > 0:
                finish(which, h - 1)
    return [
        jnp.concatenate([jnp.concatenate(across, axis=1) for across in lines], axis=0)
        for lines in tiles
    ]


def pair_kernel(
    step_angle,
    row_hbm,
    blocks_hbm,
    covered_hbm,
    weights_ref,
    slots_ref,
    codes_ref,
    total_ref,
    row_ref,
    blocks_ref,
    covered_ref,
    load_sem,
):
    me = lax.axis_index("pt")
    blocks_here = weights_ref.shape[0]
    rows = slots_ref.shape[0]
    later = codes_ref.shape[0] - 1
    lowest = me * blocks_here

    @pl.when(codes_ref[0, 0, 0] > later)
    def _():
        loads = [
            pltpu.make_async_copy(source, target, load_sem.at[k])
            for k, (source, target) in enumerate(
                ((row_hbm, row_ref), (blocks_hbm, blocks_ref), (covered_hbm, covered_ref))
            )
        ]
        for copy in loads:
            copy.start()
        total_ref[...] = jnp.zeros_like(total_ref)
        for copy in loads:
            copy.wait()

        def one_row(row, seen):
            rupture = row_ref[row]

            def one_slot(slot, carry):
                found, seen = carry
                local = blocks_ref[rupture, slot] - lowest
                live = (local >= 0) & (local < blocks_here)

                def add(sums):
                    spectra = pair_spectrum(
                        step_angle, slots_ref, weights_ref, sums, row, found, local
                    )
                    for which, spectrum in enumerate(spectra):
                        total_ref[row, which] += spectrum

                @pl.when(live & (seen >= later))
                def _():
                    with_sums(add)

                return found + live.astype(jnp.int32), seen + live.astype(jnp.int32)

            return lax.fori_loop(0, covered_ref[rupture], one_slot, (jnp.int32(0), seen))[1]

        lax.fori_loop(0, rows, one_row, jnp.int32(0))


def merge_kernel(
    count,
    step_angle,
    begun_ref,
    codes_ref,
    slots_ref,
    weights_ref,
    weight_ref,
    spectrum_ref,
    band_ref,
    table_ref,
    out_ref,
    total_ref,
    partial_ref,
    arrived,
    send_sem,
    recv_sem,
):
    me = lax.axis_index("pt")
    part = lax.axis_index("cmp")
    blocks_here = weights_ref.shape[0]
    rows, halves, variations, columns = begun_ref.shape
    parts = weight_ref.shape[0]
    bins = columns // 2
    friends = []
    for peer in others(me, count):
        friends += [{"pt": peer, "cmp": 0}, {"pt": peer, "cmp": 1}]
    friends.append({"pt": me, "cmp": 1 - part})
    hail(friends)
    later = codes_ref.shape[0] - 1
    begun = codes_ref[0, 0, 0] > later
    total_ref[...] = jnp.where(begun, begun_ref[...], 0.0)

    def first_pairs(sums):
        for j in range(later):
            code = codes_ref[j + 1, 0, 0]
            safe = jnp.maximum(code, 0)
            holder = lax.div(safe, blocks_here)
            row = lax.div(holder, blocks_here)
            spectra = pair_spectrum(
                step_angle,
                slots_ref,
                weights_ref,
                sums,
                row,
                safe - holder * blocks_here,
                holder - row * blocks_here,
            )
            chosen = jnp.where(code < 0, -1, row)
            for other in range(rows):
                share = jnp.where(chosen == other, 1.0, 0.0)
                for which in range(halves):
                    total_ref[other, which] += share * spectra[which]

    with_sums(first_pairs)
    partial_ref[...] = total_ref[...].astype(partial_ref.dtype)
    await_all(friends)
    sends = []
    for step, friend in enumerate(friends):
        copy = pltpu.make_async_remote_copy(
            src_ref=partial_ref.at[friend["pt"]],
            dst_ref=arrived.at[me, part],
            send_sem=send_sem.at[step],
            recv_sem=recv_sem.at[me, part],
            device_id=friend,
            device_id_type=MESH,
        )
        copy.start()
        sends.append(copy)
    steps = pl.ds(pl.multiple_of(part * out_ref.shape[3], out_ref.shape[3]), out_ref.shape[3])

    def finish(sums):
        for q in range(parts):
            for fine in range(2):
                pltpu.matmul_push_rhs(table_ref[q, fine, steps, :], q, fine, transpose=True)
        arrived[me, part] = partial_ref[me]
        for friend in friends:
            arrival = arrived.at[friend["pt"], friend["cmp"]]
            pltpu.make_async_remote_copy(
                src_ref=arrival,
                dst_ref=arrival,
                send_sem=send_sem.at[0],
                recv_sem=recv_sem.at[friend["pt"], friend["cmp"]],
                device_id=friend,
                device_id_type=MESH,
            ).wait_recv()
        for q in range(parts):
            total = arrived[0, q].astype(jnp.float32)
            for source in range(1, count):
                total = total + arrived[source, q].astype(jnp.float32)
            excess = []
            for c in range(2):
                lanes = slice(c * bins, (c + 1) * bins)
                whole = jnp.concatenate([total[which][:, lanes] for which in range(halves)], axis=1)
                here = pl.ds(c * variations, variations)
                excess.append((whole - spectrum_ref[q, here, :]) * weight_ref[q])
            rows_here = jnp.concatenate(excess, axis=0)
            head = rows_here.astype(jnp.bfloat16)
            tail = (rows_here - head.astype(jnp.float32)).astype(jnp.bfloat16)
            pltpu.matmul_acc_lhs(sums[0], jnp.concatenate([head, tail], axis=0), load_staged_rhs=q)
            pltpu.matmul_acc_lhs(sums[1], head, load_staged_rhs=q)
        coarse = pltpu.matmul_pop(sums[0])
        depth = 2 * variations
        low = band_ref[0] + (coarse[:depth] + (coarse[depth:] + pltpu.matmul_pop(sums[1])))
        for c in range(2):
            out_ref[0, :, c, :] = low[c * variations : (c + 1) * variations]

    pl.run_scoped(
        lambda *sums: finish(sums),
        pltpu.ACC(0)((4 * variations, 256), jnp.float32),
        pltpu.ACC(1)((2 * variations, 256), jnp.float32),
    )
    for copy in sends:
        copy.wait_send()


def final_kernel(low_ref, out_ref):
    out_ref[...] = low_ref[...]


def stay(array):
    return pltpu.with_memory_space_constraint(array, VMEM)


def body(
    strain_green,
    green_scale,
    mechanism,
    slip_amplitude,
    onset_time,
    rupture_row,
    rupture_blocks,
    block_count,
    crossover,
    high_band,
):
    points, parts_of, bins = strain_green.shape
    blocks_here = green_scale.shape[0]
    block = points // blocks_here
    rows_here, variations, slots = slip_amplitude.shape
    count = lax.axis_size("pt")
    parts = lax.axis_size("cmp")
    own = high_band.shape[3]
    samples = own * parts
    rows = rows_here * count
    tables = jnp.asarray(basis_tables(bins, parts, samples))
    spread, own_terms = spread_tables(parts_of, mechanism.shape[0], 8)
    vmem = pl.BlockSpec(memory_space=VMEM)
    smem = pl.BlockSpec(memory_space=SMEM)
    anywhere = pl.BlockSpec(memory_space=pltpu.HBM)
    grant = 24 * 1024 * 1024
    later = 5
    step_angle = 2.0 * math.pi / samples
    share = (blocks_here, 2, variations, block)
    weights, slots_all, bands, table, weight, band_spectrum, codes = pl.pallas_call(
        functools.partial(gather_kernel, count),
        out_shape=(
            VMEM((blocks_here, 2, 2 * block, 2 * bins), jnp.bfloat16),
            VMEM((rows,) + share, jnp.int16),
            VMEM((2, 2 * variations, own), jnp.float32),
            VMEM(tables.shape, jnp.bfloat16),
            VMEM((parts, variations, 2 * bins), jnp.float32),
            VMEM((parts, 2 * variations, 2 * bins), jnp.float32),
            VMEM((later + 1, 8, 128), jnp.int32),
        ),
        in_specs=[anywhere] * 13,
        out_specs=(vmem,) * 7,
        scratch_shapes=[
            SMEM(rupture_row.shape, jnp.int32),
            SMEM(rupture_blocks.shape, jnp.int32),
            SMEM(block_count.shape, jnp.int32),
            SMEM(crossover.shape, jnp.int32),
            VMEM(spread.shape, jnp.bfloat16),
            VMEM(own_terms.shape, jnp.bfloat16),
            VMEM(green_scale.shape, green_scale.dtype),
            VMEM(mechanism.shape, mechanism.dtype),
            VMEM(slip_amplitude.shape, slip_amplitude.dtype),
            VMEM(onset_time.shape, onset_time.dtype),
            VMEM(high_band.shape, high_band.dtype),
            VMEM((points * parts_of, bins), strain_green.dtype),
            VMEM((slots // block, 2, variations, block), jnp.int16),
            VMEM((count - 1,) + share, jnp.int16),
            pltpu.SemaphoreType.DMA,
            pltpu.SemaphoreType.DMA((11,)),
            pltpu.SemaphoreType.DMA((blocks_here,)),
            pltpu.SemaphoreType.DMA((count,)),
            pltpu.SemaphoreType.DMA((count + 1,)),
        ],
        compiler_params=pltpu.CompilerParams(collective_id=0, has_side_effects=True),
        name="gather",
    )(
        rupture_row,
        rupture_blocks,
        block_count,
        crossover,
        strain_green.reshape(points * parts_of, bins),
        green_scale,
        mechanism,
        slip_amplitude,
        onset_time,
        high_band,
        tables,
        jnp.asarray(spread),
        jnp.asarray(own_terms),
    )
    begun = pl.pallas_call(
        functools.partial(pair_kernel, step_angle),
        out_shape=VMEM((rows, 2, variations, 2 * bins), jnp.float32),
        in_specs=[anywhere] * 3 + [vmem] * 3,
        out_specs=vmem,
        scratch_shapes=[
            SMEM(rupture_row.shape, jnp.int32),
            SMEM(rupture_blocks.shape, jnp.int32),
            SMEM(block_count.shape, jnp.int32),
            pltpu.SemaphoreType.DMA((3,)),
        ],
        compiler_params=pltpu.CompilerParams(vmem_limit_bytes=grant),
        name="pairs",
    )(rupture_row, rupture_blocks, block_count, stay(weights), stay(slots_all), stay(codes))
    return pl.pallas_call(
        functools.partial(merge_kernel, count, step_angle),
        out_shape=jax.ShapeDtypeStruct(high_band.shape, high_band.dtype),
        in_specs=[vmem] * 8,
        out_specs=vmem,
        scratch_shapes=[
            VMEM((rows, 2, variations, 2 * bins), jnp.float32),
            VMEM((rows, 2, variations, 2 * bins), jnp.bfloat16),
            VMEM((count, parts, 2, variations, 2 * bins), jnp.bfloat16),
            pltpu.SemaphoreType.DMA((2 * count - 1,)),
            pltpu.SemaphoreType.DMA((count, parts)),
        ],
        compiler_params=pltpu.CompilerParams(collective_id=1, has_side_effects=True, vmem_limit_bytes=grant),
        name="merge",
    )(stay(begun), stay(codes), stay(slots_all), stay(weights), stay(weight), stay(band_spectrum), stay(bands), stay(table))


def solution(mesh):
    return jax.shard_map(
        body,
        mesh=mesh,
        in_specs=(
            P(("site", "pt"), None, "cmp"),
            P(("site", "pt"), None),
            P(None, "pt"),
            P("pt", "var", None),
            P("pt", "var", None),
            P(),
            P(),
            P(),
            P(),
            P(("site", "pt"), "var", None, "cmp"),
        ),
        out_specs=P(("site", "pt"), "var", None, "cmp"),
        check_vma=False,
    )
```

```python
import functools
import math

import jax
import jax.numpy as jnp
import numpy as np
from jax import lax
from jax.experimental import pallas as pl
from jax.experimental.pallas import tpu as pltpu
from jax.sharding import PartitionSpec as P

taper_width = 8.0
onset_middle = 64.0
onset_steps = 512.0
slip_steps = 1024.0
MESH = pl.DeviceIdType.MESH
VMEM = pltpu.VMEM
SMEM = pltpu.SMEM


def column_bins(bins_here):
    half = bins_here // 2
    column = np.arange(2 * bins_here)
    return (column // bins_here) * half + column % half, (column // half) % 2


def basis_tables(bins_here, parts, samples):
    bins, imaginary = column_bins(bins_here)
    time = np.arange(samples)[:, None]
    tables = []
    for part in range(parts):
        angle = ((part * bins_here + bins)[None, :] * time % samples) * (2.0 * math.pi / samples)
        tables.append(np.where(imaginary[None, :] == 1, -np.sin(angle), np.cos(angle)))
    exact = np.stack(tables)
    upper = exact.astype(jnp.bfloat16)
    lower = (exact - upper.astype(np.float64)).astype(jnp.bfloat16)
    return np.stack([upper, lower], axis=1)


def spread_tables(parts_of, terms, group):
    depth = group * parts_of
    column = np.arange(depth)
    spread = (np.arange(parts_of)[:, None] == column[None, :] % parts_of).astype(jnp.bfloat16)
    quarter = np.arange(parts_of // terms * group)
    own_point = quarter[:, None] % group == column[None, :] // parts_of
    own_term = quarter[:, None] // group == (column[None, :] % parts_of) // terms
    return spread, (own_point & own_term).astype(jnp.bfloat16)


def wide_dot(rows, upper, lower, dims):
    head = rows.astype(jnp.bfloat16)
    tail = (rows - head.astype(jnp.float32)).astype(jnp.bfloat16)
    dot = functools.partial(
        lax.dot_general, dimension_numbers=(dims, ((), ())), preferred_element_type=jnp.float32
    )
    return dot(head, upper) + (dot(head, lower) + dot(tail, upper))


def hail(peers):
    barrier = pltpu.get_barrier_semaphore()
    for peer in peers:
        pl.semaphore_signal(barrier, inc=1, device_id=peer, device_id_type=MESH)


def await_all(peers):
    pl.semaphore_wait(pltpu.get_barrier_semaphore(), len(peers))


def greet(peers):
    hail(peers)
    await_all(peers)


def others(me, count):
    sense = jnp.where(2 * me < count, count - 1, 1)
    return [lax.rem(me + sense * step, count) for step in range(1, count)]


def gather_kernel(
    count,
    row_hbm,
    blocks_hbm,
    covered_hbm,
    crossover_hbm,
    strain_ref,
    scale_hbm,
    mechanism_hbm,
    slip_hbm,
    onset_hbm,
    band_hbm,
    table_hbm,
    spread_hbm,
    own_hbm,
    weights_ref,
    slots_ref,
    band_both,
    table_ref,
    weight_ref,
    spectrum_ref,
    codes_ref,
    row_ref,
    blocks_ref,
    covered_ref,
    crossover_ref,
    spread_ref,
    own_ref,
    scale_ref,
    mechanism_ref,
    slip_ref,
    onset_ref,
    band_ref,
    strain_buf,
    coded_ref,
    slot_pack,
    local_sem,
    load_sem,
    strain_sem,
    send_sem,
    recv_sem,
):
    me = lax.axis_index("pt")
    part = lax.axis_index("cmp")
    partner = {"cmp": 1 - part}
    blocks_here = scale_ref.shape[0]
    parts_of = scale_ref.shape[1]
    stretch = strain_ref.shape[0] // blocks_here
    block = stretch // parts_of
    bins = strain_ref.shape[1]
    half = bins // 2
    own = band_ref.shape[3]
    variations = band_ref.shape[1]
    samples = own * table_ref.shape[0]
    peers = others(me, count)
    friends = [{"pt": peer} for peer in peers] + [partner]
    hail(friends)
    loads = []
    for k, (source, target) in enumerate(
        (
            (row_hbm, row_ref),
            (blocks_hbm, blocks_ref),
            (covered_hbm, covered_ref),
            (slip_hbm, slip_ref),
            (onset_hbm, onset_ref),
            (band_hbm, band_ref),
            (mechanism_hbm, mechanism_ref),
            (scale_hbm, scale_ref),
            (spread_hbm, spread_ref),
            (own_hbm, own_ref),
            (crossover_hbm, crossover_ref),
        )
    ):
        copy = pltpu.make_async_copy(source, target, load_sem.at[k])
        copy.start()
        loads.append(copy)
    def strain_rows(b):
        return strain_ref.at[pl.ds(pl.multiple_of(b * stretch, stretch), stretch)]

    for b in range(blocks_here):
        pltpu.make_async_copy(strain_rows(b), strain_buf.at[pl.ds(b * stretch, stretch)], strain_sem.at[b]).start()
    table_copy = pltpu.make_async_copy(table_hbm, table_ref, local_sem)
    table_copy.start()
    for copy in loads[:3]:
        copy.wait()
    rupture = row_ref[me]
    covered = covered_ref[rupture]
    spread = variations // 2

    slot_total = blocks_ref.shape[1]

    def chosen(target):
        lowest = target * blocks_here
        slots = [jnp.int32(0)] * blocks_here
        found = jnp.int32(0)
        for slot in range(slot_total):
            named = blocks_ref[rupture, slot]
            live = (slot < covered) & (named >= lowest) & (named < lowest + blocks_here)
            for k in range(min(blocks_here, slot + 1)):
                slots[k] = jnp.where(live & (found == k), slot, slots[k])
            found = found + live.astype(jnp.int32)
        return slots

    sent = [chosen(peer) for peer in peers]
    kept = chosen(me)
    for copy in loads[3:5]:
        copy.wait()
    for slot in range(slot_total):
        lanes = pl.ds(slot * block, block)
        onset = (onset_ref[0, :, lanes] - onset_middle) * onset_steps
        onset = jnp.minimum(jnp.round(onset), onset_middle * onset_steps - 1.0)
        slip = slip_ref[0, :, lanes].astype(jnp.float32) * slip_steps
        for h in range(2):
            lines = slice(h * spread, (h + 1) * spread)
            coded_ref[slot, h] = (
                jnp.concatenate([onset[lines], slip[lines]], axis=0)
                .astype(jnp.int32)
                .astype(coded_ref.dtype)
            )

    for step, slots in enumerate(sent):
        for k, slot in enumerate(slots):
            slot_pack[step, k] = coded_ref[slot]
    await_all(friends)
    sends = []
    for step, peer in enumerate(peers):
        copy = pltpu.make_async_remote_copy(
            src_ref=slot_pack.at[step],
            dst_ref=slots_ref.at[me],
            send_sem=send_sem.at[step],
            recv_sem=recv_sem.at[me],
            device_id={"pt": peer},
            device_id_type=MESH,
        )
        copy.start()
        sends.append(copy)
    loads[5].wait()
    for c in range(2):
        band_both[0, pl.ds(c * variations, variations), :] = band_ref[0, :, c, :]
    band_copy = pltpu.make_async_remote_copy(
        src_ref=band_both.at[0],
        dst_ref=band_both.at[1],
        send_sem=send_sem.at[count - 1],
        recv_sem=recv_sem.at[count],
        device_id=partner,
        device_id_type=MESH,
    )
    band_copy.start()
    for k, slot in enumerate(kept):
        slots_ref[me, k] = coded_ref[slot]

    for copy in loads[6:]:
        copy.wait()
    crossing = crossover_ref[rupture].astype(jnp.float32)
    column = lax.broadcasted_iota(jnp.int32, weight_ref.shape[1:], 1)
    for q in range(weight_ref.shape[0]):
        frequency_id = q * bins + (column // bins) * half + column % half
        frequency = frequency_id.astype(jnp.float32)
        taper = jnp.clip((crossing - frequency) / taper_width + 0.5, 0.0, 1.0)
        weight_ref[q] = taper * jnp.where(frequency_id == 0, 1.0, 2.0) / samples
    group = 8
    pair = 2 * group
    depth = group * parts_of
    low_lanes = lax.broadcasted_iota(jnp.int32, (pair, bins), 1) < half
    dot = functools.partial(jnp.dot, preferred_element_type=jnp.float32)

    def make_block(b, carry):
        pltpu.make_async_copy(strain_rows(b), strain_buf.at[pl.ds(b * stretch, stretch)], strain_sem.at[b]).wait()
        moment = mechanism_ref[:, pl.ds(pl.multiple_of(b * block, block), block)]
        factors = jnp.transpose(jnp.concatenate([moment] * 4, axis=0)) * scale_ref[pl.ds(b, 1), :]
        head = factors.astype(jnp.bfloat16)
        tail = (factors - head.astype(jnp.float32)).astype(jnp.bfloat16)
        wide = [dot(piece, spread_ref[...]) for piece in (head, tail)]
        for first in range(0, block, pair):
            sums = []
            for start in (first, first + group):
                rows = []
                for piece in wide:
                    tile = piece[start : start + group]
                    twice = jnp.concatenate([tile, tile], axis=0).astype(jnp.bfloat16)
                    rows += [twice * own_ref[:pair], twice * own_ref[pair:]]
                product = dot(
                    jnp.concatenate(rows, axis=0),
                    strain_buf[pl.ds(pl.multiple_of(b * stretch + start * parts_of, depth), depth), :],
                )
                sums.append(product[: 2 * pair] + product[2 * pair :])
            quarters = [
                jnp.concatenate([part_sum[q * group : (q + 1) * group] for part_sum in sums], axis=0)
                for q in range(4)
            ]
            for c in range(2):
                real, imag = quarters[c], quarters[2 + c]
                real_turned = pltpu.roll(real, half, 1)
                imag_turned = pltpu.roll(imag, half, 1)
                lanes = pl.ds(c * bins, bins)
                pieces = (
                    (0, 0, real, imag_turned),
                    (0, 1, imag, -real_turned),
                    (1, 0, real_turned, imag),
                    (1, 1, imag_turned, -real),
                )
                for which, lower, first_half, second_half in pieces:
                    weights_ref[b, which, pl.ds(lower * block + first, pair), lanes] = jnp.where(
                        low_lanes, first_half, second_half
                    ).astype(jnp.bfloat16)
        return carry

    lax.fori_loop(0, blocks_here, make_block, 0)

    later = codes_ref.shape[0] - 1
    lowest = me * blocks_here

    def list_row(row, carry):
        seen, codes = carry[0], list(carry[1:])
        covered_here = covered_ref[row_ref[row]]
        found = jnp.int32(0)
        for slot in range(slot_total):
            local = blocks_ref[row_ref[row], slot] - lowest
            live = (slot < covered_here) & (local >= 0) & (local < blocks_here)
            code = (row * blocks_here + local) * blocks_here + found
            for j in range(later):
                codes[j] = jnp.where(live & (seen == j), code, codes[j])
            found = found + live.astype(jnp.int32)
            seen = seen + live.astype(jnp.int32)
        return (seen, *codes)

    seen, *codes = lax.fori_loop(
        0, slots_ref.shape[0], list_row, (jnp.int32(0),) + (jnp.int32(-1),) * later
    )
    for j, code in enumerate([seen] + codes):
        codes_ref[j] = jnp.full(codes_ref.shape[1:], code, jnp.int32)
    table_copy.wait()
    band_copy.wait()
    down = ((1,), (0,))
    lines = [pl.ds(pl.multiple_of(lax.rem(part + k, 2) * own, own), own) for k in range(2)]
    bands = [
        wide_dot(band_both[0], table_ref[q, 0, lines[0], :], table_ref[q, 1, lines[0], :], down)
        + wide_dot(band_both[1], table_ref[q, 0, lines[1], :], table_ref[q, 1, lines[1], :], down)
        for q in range(spectrum_ref.shape[0])
    ]
    for q, band in enumerate(bands):
        spectrum_ref[q] = band
    for copy in sends:
        copy.wait_send()
    for peer in peers:
        arrival = slots_ref.at[peer]
        pltpu.make_async_remote_copy(
            src_ref=arrival,
            dst_ref=arrival,
            send_sem=send_sem.at[0],
            recv_sem=recv_sem.at[peer],
            device_id={"pt": peer},
            device_id_type=MESH,
        ).wait_recv()


def turn(first, second):
    return (
        first[0] * second[0] - first[1] * second[1],
        first[0] * second[1] + first[1] * second[0],
    )


def quarter_unit(angle):
    off = angle - 0.25 * math.pi
    square = off * off
    sine = off * (
        1.0
        + square * (-1.0 / 6 + square * (1.0 / 120 + square * (-1.0 / 5040 + square * (1.0 / 362880))))
    )
    cosine = 1.0 + square * (
        -0.5
        + square
        * (1.0 / 24 + square * (-1.0 / 720 + square * (1.0 / 40320 + square * (-1.0 / 3628800))))
    )
    scale = math.sqrt(0.5)
    return scale * (cosine - sine), scale * (cosine + sine)


def slot_rows(slots_ref, row, found, spread):
    pieces = [
        slots_ref[row, found, h].astype(jnp.int32).astype(jnp.float32)
        for h in range(slots_ref.shape[2])
    ]
    onset = jnp.concatenate([piece[:spread] for piece in pieces], axis=0)
    slip = jnp.concatenate([piece[spread:] for piece in pieces], axis=0)
    return onset / onset_steps + onset_middle, slip / slip_steps


def with_sums(action):
    units = [pltpu.ACC(unit)((256, 256), jnp.float32) for unit in (0, 0, 1, 1)]
    pl.run_scoped(lambda *sums: action((sums[:2], sums[2:])), *units)


def pair_spectrum(step_angle, slots_ref, weights_ref, sums, row, found, local):
    halves, depth, columns = weights_ref.shape[1:]
    spread = slots_ref.shape[3] // 2
    bins = columns // 2
    half = bins // 2
    fine_total = 16
    reach = fine_total // 2
    onset, slip = slot_rows(slots_ref, row, found, spread)
    variations = onset.shape[0]
    powers = [None, quarter_unit(step_angle * onset)]
    for k in range(2, reach + 1):
        powers.append(turn(powers[k // 2], powers[k - k // 2]))
    leap = turn(powers[reach], powers[reach])
    far = leap
    for unused in range(int(math.log2(bins // fine_total))):
        far = turn(far, far)
    second_part = lax.axis_index("cmp") == 1
    centre = turn(
        powers[reach],
        (slip * jnp.where(second_part, far[0], 1.0), slip * jnp.where(second_part, far[1], 0.0)),
    )
    rounds = half // fine_total
    centres = [centre]
    for unused in range(halves * rounds - 1):
        centres.append(turn(centres[-1], leap))
    for which in range(halves):
        pltpu.matmul_push_rhs(weights_ref[local, which], 0, which)
    lane_bin = lax.broadcasted_iota(jnp.int32, (8, 128), 1) % half
    tiles = [
        [
            [jnp.zeros((8, 128), jnp.float32) for lane in range(columns // 128)]
            for line in range(variations // 8)
        ]
        for which in range(halves)
    ]

    def start(which, h):
        middle = centres[which * rounds + h]
        near = [None] * fine_total
        near[reach] = middle
        for k in range(1, reach + 1):
            cos_cos, sin_sin = middle[0] * powers[k][0], middle[1] * powers[k][1]
            sin_cos, cos_sin = middle[1] * powers[k][0], middle[0] * powers[k][1]
            near[reach - k] = (cos_cos + sin_sin, sin_cos - cos_sin)
            if k < reach:
                near[reach + k] = (cos_cos - sin_sin, sin_cos + cos_sin)
        pieces = [
            jnp.concatenate([phase[0].astype(jnp.bfloat16), phase[1].astype(jnp.bfloat16)], axis=1)
            for phase in near
        ]
        pltpu.matmul_acc_lhs(
            sums[which][h % 2], jnp.concatenate(pieces, axis=0), load_staged_rhs=0 if h == 0 else None
        )

    def finish(which, h):
        product = pltpu.matmul_pop(sums[which][h % 2])
        for k in range(fine_total):
            here = lane_bin == h * fine_total + k
            for line, across in enumerate(tiles[which]):
                first = k * variations + 8 * line
                for lane in range(len(across)):
                    across[lane] = jnp.where(
                        here, product[first : first + 8, 128 * lane : 128 * (lane + 1)], across[lane]
                    )

    for h in range(rounds + 1):
        for which in range(halves):
            if h < rounds:
                start(which, h)
            if h > 0:
                finish(which, h - 1)
    return [
        jnp.concatenate([jnp.concatenate(across, axis=1) for across in lines], axis=0)
        for lines in tiles
    ]


def pair_kernel(
    step_angle,
    row_hbm,
    blocks_hbm,
    covered_hbm,
    weights_ref,
    slots_ref,
    codes_ref,
    total_ref,
    row_ref,
    blocks_ref,
    covered_ref,
    load_sem,
):
    me = lax.axis_index("pt")
    blocks_here = weights_ref.shape[0]
    rows = slots_ref.shape[0]
    later = codes_ref.shape[0] - 1
    lowest = me * blocks_here

    @pl.when(codes_ref[0, 0, 0] > later)
    def _():
        loads = [
            pltpu.make_async_copy(source, target, load_sem.at[k])
            for k, (source, target) in enumerate(
                ((row_hbm, row_ref), (blocks_hbm, blocks_ref), (covered_hbm, covered_ref))
            )
        ]
        for copy in loads:
            copy.start()
        total_ref[...] = jnp.zeros_like(total_ref)
        for copy in loads:
            copy.wait()

        def one_row(row, seen):
            rupture = row_ref[row]

            def one_slot(slot, carry):
                found, seen = carry
                local = blocks_ref[rupture, slot] - lowest
                live = (local >= 0) & (local < blocks_here)

                def add(sums):
                    spectra = pair_spectrum(
                        step_angle, slots_ref, weights_ref, sums, row, found, local
                    )
                    for which, spectrum in enumerate(spectra):
                        total_ref[row, which] += spectrum

                @pl.when(live & (seen >= later))
                def _():
                    with_sums(add)

                return found + live.astype(jnp.int32), seen + live.astype(jnp.int32)

            return lax.fori_loop(0, covered_ref[rupture], one_slot, (jnp.int32(0), seen))[1]

        lax.fori_loop(0, rows, one_row, jnp.int32(0))


def merge_kernel(
    count,
    step_angle,
    begun_ref,
    codes_ref,
    slots_ref,
    weights_ref,
    weight_ref,
    spectrum_ref,
    band_ref,
    table_ref,
    out_ref,
    total_ref,
    partial_ref,
    arrived,
    send_sem,
    recv_sem,
):
    me = lax.axis_index("pt")
    part = lax.axis_index("cmp")
    blocks_here = weights_ref.shape[0]
    rows, halves, variations, columns = begun_ref.shape
    parts = weight_ref.shape[0]
    bins = columns // 2
    friends = []
    for peer in others(me, count):
        friends += [{"pt": peer, "cmp": 0}, {"pt": peer, "cmp": 1}]
    friends.append({"pt": me, "cmp": 1 - part})
    hail(friends)
    later = codes_ref.shape[0] - 1
    begun = codes_ref[0, 0, 0] > later
    total_ref[...] = jnp.where(begun, begun_ref[...], 0.0)

    def first_pairs(sums):
        for j in range(later):
            code = codes_ref[j + 1, 0, 0]
            safe = jnp.maximum(code, 0)
            holder = lax.div(safe, blocks_here)
            row = lax.div(holder, blocks_here)
            spectra = pair_spectrum(
                step_angle,
                slots_ref,
                weights_ref,
                sums,
                row,
                safe - holder * blocks_here,
                holder - row * blocks_here,
            )
            chosen = jnp.where(code < 0, -1, row)
            for other in range(rows):
                share = jnp.where(chosen == other, 1.0, 0.0)
                for which in range(halves):
                    total_ref[other, which] += share * spectra[which]

    with_sums(first_pairs)
    partial_ref[...] = total_ref[...].astype(partial_ref.dtype)
    await_all(friends)
    sends = []
    for step, friend in enumerate(friends):
        copy = pltpu.make_async_remote_copy(
            src_ref=partial_ref.at[friend["pt"]],
            dst_ref=arrived.at[me, part],
            send_sem=send_sem.at[step],
            recv_sem=recv_sem.at[me, part],
            device_id=friend,
            device_id_type=MESH,
        )
        copy.start()
        sends.append(copy)
    steps = pl.ds(pl.multiple_of(part * out_ref.shape[3], out_ref.shape[3]), out_ref.shape[3])

    def finish(sums):
        for q in range(parts):
            for fine in range(2):
                pltpu.matmul_push_rhs(table_ref[q, fine, steps, :], q, fine, transpose=True)
        arrived[me, part] = partial_ref[me]
        for friend in friends:
            arrival = arrived.at[friend["pt"], friend["cmp"]]
            pltpu.make_async_remote_copy(
                src_ref=arrival,
                dst_ref=arrival,
                send_sem=send_sem.at[0],
                recv_sem=recv_sem.at[friend["pt"], friend["cmp"]],
                device_id=friend,
                device_id_type=MESH,
            ).wait_recv()
        for q in range(parts):
            total = arrived[0, q].astype(jnp.float32)
            for source in range(1, count):
                total = total + arrived[source, q].astype(jnp.float32)
            excess = []
            for c in range(2):
                lanes = slice(c * bins, (c + 1) * bins)
                whole = jnp.concatenate([total[which][:, lanes] for which in range(halves)], axis=1)
                here = pl.ds(c * variations, variations)
                excess.append((whole - spectrum_ref[q, here, :]) * weight_ref[q])
            rows_here = jnp.concatenate(excess, axis=0)
            head = rows_here.astype(jnp.bfloat16)
            tail = (rows_here - head.astype(jnp.float32)).astype(jnp.bfloat16)
            pltpu.matmul_acc_lhs(sums[0], jnp.concatenate([head, tail], axis=0), load_staged_rhs=q)
            pltpu.matmul_acc_lhs(sums[1], head, load_staged_rhs=q)
        coarse = pltpu.matmul_pop(sums[0])
        depth = 2 * variations
        low = band_ref[0] + (coarse[:depth] + (coarse[depth:] + pltpu.matmul_pop(sums[1])))
        for c in range(2):
            out_ref[0, :, c, :] = low[c * variations : (c + 1) * variations]

    pl.run_scoped(
        lambda *sums: finish(sums),
        pltpu.ACC(0)((4 * variations, 256), jnp.float32),
        pltpu.ACC(1)((2 * variations, 256), jnp.float32),
    )
    for copy in sends:
        copy.wait_send()


def final_kernel(low_ref, out_ref):
    out_ref[...] = low_ref[...]


def stay(array):
    return pltpu.with_memory_space_constraint(array, VMEM)


def body(
    strain_green,
    green_scale,
    mechanism,
    slip_amplitude,
    onset_time,
    rupture_row,
    rupture_blocks,
    block_count,
    crossover,
    high_band,
):
    points, parts_of, bins = strain_green.shape
    blocks_here = green_scale.shape[0]
    block = points // blocks_here
    rows_here, variations, slots = slip_amplitude.shape
    count = lax.axis_size("pt")
    parts = lax.axis_size("cmp")
    own = high_band.shape[3]
    samples = own * parts
    rows = rows_here * count
    tables = jnp.asarray(basis_tables(bins, parts, samples))
    spread, own_terms = spread_tables(parts_of, mechanism.shape[0], 8)
    vmem = pl.BlockSpec(memory_space=VMEM)
    smem = pl.BlockSpec(memory_space=SMEM)
    anywhere = pl.BlockSpec(memory_space=pltpu.HBM)
    grant = 24 * 1024 * 1024
    later = 6
    step_angle = 2.0 * math.pi / samples
    share = (blocks_here, 2, variations, block)
    weights, slots_all, bands, table, weight, band_spectrum, codes = pl.pallas_call(
        functools.partial(gather_kernel, count),
        out_shape=(
            VMEM((blocks_here, 2, 2 * block, 2 * bins), jnp.bfloat16),
            VMEM((rows,) + share, jnp.int16),
            VMEM((2, 2 * variations, own), jnp.float32),
            VMEM(tables.shape, jnp.bfloat16),
            VMEM((parts, variations, 2 * bins), jnp.float32),
            VMEM((parts, 2 * variations, 2 * bins), jnp.float32),
            VMEM((later + 1, 8, 128), jnp.int32),
        ),
        in_specs=[anywhere] * 13,
        out_specs=(vmem,) * 7,
        scratch_shapes=[
            SMEM(rupture_row.shape, jnp.int32),
            SMEM(rupture_blocks.shape, jnp.int32),
            SMEM(block_count.shape, jnp.int32),
            SMEM(crossover.shape, jnp.int32),
            VMEM(spread.shape, jnp.bfloat16),
            VMEM(own_terms.shape, jnp.bfloat16),
            VMEM(green_scale.shape, green_scale.dtype),
            VMEM(mechanism.shape, mechanism.dtype),
            VMEM(slip_amplitude.shape, slip_amplitude.dtype),
            VMEM(onset_time.shape, onset_time.dtype),
            VMEM(high_band.shape, high_band.dtype),
            VMEM((points * parts_of, bins), strain_green.dtype),
            VMEM((slots // block, 2, variations, block), jnp.int16),
            VMEM((count - 1,) + share, jnp.int16),
            pltpu.SemaphoreType.DMA,
            pltpu.SemaphoreType.DMA((11,)),
            pltpu.SemaphoreType.DMA((blocks_here,)),
            pltpu.SemaphoreType.DMA((count,)),
            pltpu.SemaphoreType.DMA((count + 1,)),
        ],
        compiler_params=pltpu.CompilerParams(collective_id=0, has_side_effects=True),
        name="gather",
    )(
        rupture_row,
        rupture_blocks,
        block_count,
        crossover,
        strain_green.reshape(points * parts_of, bins),
        green_scale,
        mechanism,
        slip_amplitude,
        onset_time,
        high_band,
        tables,
        jnp.asarray(spread),
        jnp.asarray(own_terms),
    )
    begun = pl.pallas_call(
        functools.partial(pair_kernel, step_angle),
        out_shape=VMEM((rows, 2, variations, 2 * bins), jnp.float32),
        in_specs=[anywhere] * 3 + [vmem] * 3,
        out_specs=vmem,
        scratch_shapes=[
            SMEM(rupture_row.shape, jnp.int32),
            SMEM(rupture_blocks.shape, jnp.int32),
            SMEM(block_count.shape, jnp.int32),
            pltpu.SemaphoreType.DMA((3,)),
        ],
        compiler_params=pltpu.CompilerParams(vmem_limit_bytes=grant),
        name="pairs",
    )(rupture_row, rupture_blocks, block_count, stay(weights), stay(slots_all), stay(codes))
    return pl.pallas_call(
        functools.partial(merge_kernel, count, step_angle),
        out_shape=jax.ShapeDtypeStruct(high_band.shape, high_band.dtype),
        in_specs=[vmem] * 8,
        out_specs=vmem,
        scratch_shapes=[
            VMEM((rows, 2, variations, 2 * bins), jnp.float32),
            VMEM((rows, 2, variations, 2 * bins), jnp.bfloat16),
            VMEM((count, parts, 2, variations, 2 * bins), jnp.bfloat16),
            pltpu.SemaphoreType.DMA((2 * count - 1,)),
            pltpu.SemaphoreType.DMA((count, parts)),
        ],
        compiler_params=pltpu.CompilerParams(collective_id=1, has_side_effects=True, vmem_limit_bytes=grant),
        name="merge",
    )(stay(begun), stay(codes), stay(slots_all), stay(weights), stay(weight), stay(band_spectrum), stay(bands), stay(table))


def solution(mesh):
    return jax.shard_map(
        body,
        mesh=mesh,
        in_specs=(
            P(("site", "pt"), None, "cmp"),
            P(("site", "pt"), None),
            P(None, "pt"),
            P("pt", "var", None),
            P("pt", "var", None),
            P(),
            P(),
            P(),
            P(),
            P(("site", "pt"), "var", None, "cmp"),
        ),
        out_specs=P(("site", "pt"), "var", None, "cmp"),
        check_vma=False,
    )
```

```python
import functools
import math

import jax
import jax.numpy as jnp
import numpy as np
from jax import lax
from jax.experimental import pallas as pl
from jax.experimental.pallas import tpu as pltpu
from jax.sharding import PartitionSpec as P

taper_width = 8.0
onset_middle = 64.0
onset_steps = 512.0
slip_steps = 1024.0
MESH = pl.DeviceIdType.MESH
VMEM = pltpu.VMEM
SMEM = pltpu.SMEM


def column_bins(bins_here):
    half = bins_here // 2
    column = np.arange(2 * bins_here)
    return (column // bins_here) * half + column % half, (column // half) % 2


def basis_tables(bins_here, parts, samples):
    bins, imaginary = column_bins(bins_here)
    time = np.arange(samples)[:, None]
    tables = []
    for part in range(parts):
        angle = ((part * bins_here + bins)[None, :] * time % samples) * (2.0 * math.pi / samples)
        tables.append(np.where(imaginary[None, :] == 1, -np.sin(angle), np.cos(angle)))
    exact = np.stack(tables)
    upper = exact.astype(jnp.bfloat16)
    lower = (exact - upper.astype(np.float64)).astype(jnp.bfloat16)
    return np.stack([upper, lower], axis=1)


def spread_tables(parts_of, terms, group):
    depth = group * parts_of
    column = np.arange(depth)
    spread = (np.arange(parts_of)[:, None] == column[None, :] % parts_of).astype(np.float32)
    quarter = np.arange(parts_of // terms * group)
    own_point = quarter[:, None] % group == column[None, :] // parts_of
    own_term = quarter[:, None] // group == (column[None, :] % parts_of) // terms
    return spread, (own_point & own_term).astype(jnp.bfloat16)


def wide_dot(rows, upper, lower, dims):
    head = rows.astype(jnp.bfloat16)
    tail = (rows - head.astype(jnp.float32)).astype(jnp.bfloat16)
    dot = functools.partial(
        lax.dot_general, dimension_numbers=(dims, ((), ())), preferred_element_type=jnp.float32
    )
    return dot(head, upper) + (dot(head, lower) + dot(tail, upper))


def hail(peers):
    barrier = pltpu.get_barrier_semaphore()
    for peer in peers:
        pl.semaphore_signal(barrier, inc=1, device_id=peer, device_id_type=MESH)


def await_all(peers):
    pl.semaphore_wait(pltpu.get_barrier_semaphore(), len(peers))


def greet(peers):
    hail(peers)
    await_all(peers)


def others(me, count):
    sense = jnp.where(2 * me < count, count - 1, 1)
    return [lax.rem(me + sense * step, count) for step in range(1, count)]


def gather_kernel(
    count,
    row_hbm,
    blocks_hbm,
    covered_hbm,
    crossover_hbm,
    strain_ref,
    scale_hbm,
    mechanism_hbm,
    slip_hbm,
    onset_hbm,
    band_hbm,
    table_hbm,
    spread_hbm,
    own_hbm,
    weights_ref,
    slots_ref,
    band_both,
    table_ref,
    weight_ref,
    spectrum_ref,
    codes_ref,
    row_ref,
    blocks_ref,
    covered_ref,
    crossover_ref,
    spread_ref,
    own_ref,
    scale_ref,
    mechanism_ref,
    slip_ref,
    onset_ref,
    band_ref,
    strain_buf,
    coded_ref,
    slot_pack,
    local_sem,
    load_sem,
    strain_sem,
    send_sem,
    recv_sem,
):
    me = lax.axis_index("pt")
    part = lax.axis_index("cmp")
    partner = {"cmp": 1 - part}
    blocks_here = scale_ref.shape[0]
    parts_of = scale_ref.shape[1]
    stretch = strain_ref.shape[0] // blocks_here
    block = stretch // parts_of
    bins = strain_ref.shape[1]
    half = bins // 2
    own = band_ref.shape[3]
    variations = band_ref.shape[1]
    samples = own * table_ref.shape[0]
    peers = others(me, count)
    friends = [{"pt": peer} for peer in peers] + [partner]
    hail(friends)
    loads = []
    for k, (source, target) in enumerate(
        (
            (row_hbm, row_ref),
            (blocks_hbm, blocks_ref),
            (covered_hbm, covered_ref),
            (slip_hbm, slip_ref),
            (onset_hbm, onset_ref),
            (band_hbm, band_ref),
            (mechanism_hbm, mechanism_ref),
            (scale_hbm, scale_ref),
            (spread_hbm, spread_ref),
            (own_hbm, own_ref),
            (crossover_hbm, crossover_ref),
        )
    ):
        copy = pltpu.make_async_copy(source, target, load_sem.at[k])
        copy.start()
        loads.append(copy)
    def strain_rows(b):
        return strain_ref.at[pl.ds(pl.multiple_of(b * stretch, stretch), stretch)]

    for b in range(blocks_here):
        pltpu.make_async_copy(strain_rows(b), strain_buf.at[pl.ds(b * stretch, stretch)], strain_sem.at[b]).start()
    table_copy = pltpu.make_async_copy(table_hbm, table_ref, local_sem)
    table_copy.start()
    for copy in loads[:3]:
        copy.wait()
    rupture = row_ref[me]
    covered = covered_ref[rupture]
    spread = variations // 2

    slot_total = blocks_ref.shape[1]

    def chosen(target):
        lowest = target * blocks_here
        slots = [jnp.int32(0)] * blocks_here
        found = jnp.int32(0)
        for slot in range(slot_total):
            named = blocks_ref[rupture, slot]
            live = (slot < covered) & (named >= lowest) & (named < lowest + blocks_here)
            for k in range(min(blocks_here, slot + 1)):
                slots[k] = jnp.where(live & (found == k), slot, slots[k])
            found = found + live.astype(jnp.int32)
        return slots

    sent = [chosen(peer) for peer in peers]
    kept = chosen(me)
    for copy in loads[3:5]:
        copy.wait()
    for slot in range(slot_total):
        lanes = pl.ds(slot * block, block)
        onset = (onset_ref[0, :, lanes] - onset_middle) * onset_steps
        onset = jnp.minimum(jnp.round(onset), onset_middle * onset_steps - 1.0)
        slip = slip_ref[0, :, lanes].astype(jnp.float32) * slip_steps
        for h in range(2):
            lines = slice(h * spread, (h + 1) * spread)
            coded_ref[slot, h] = (
                jnp.concatenate([onset[lines], slip[lines]], axis=0)
                .astype(jnp.int32)
                .astype(coded_ref.dtype)
            )

    for step, slots in enumerate(sent):
        for k, slot in enumerate(slots):
            slot_pack[step, k] = coded_ref[slot]
    await_all(friends)
    sends = []
    for step, peer in enumerate(peers):
        copy = pltpu.make_async_remote_copy(
            src_ref=slot_pack.at[step],
            dst_ref=slots_ref.at[me],
            send_sem=send_sem.at[step],
            recv_sem=recv_sem.at[me],
            device_id={"pt": peer},
            device_id_type=MESH,
        )
        copy.start()
        sends.append(copy)
    loads[5].wait()
    for c in range(2):
        band_both[0, pl.ds(c * variations, variations), :] = band_ref[0, :, c, :]
    band_copy = pltpu.make_async_remote_copy(
        src_ref=band_both.at[0],
        dst_ref=band_both.at[1],
        send_sem=send_sem.at[count - 1],
        recv_sem=recv_sem.at[count],
        device_id=partner,
        device_id_type=MESH,
    )
    band_copy.start()
    for k, slot in enumerate(kept):
        slots_ref[me, k] = coded_ref[slot]

    for copy in loads[6:]:
        copy.wait()
    crossing = crossover_ref[rupture].astype(jnp.float32)
    column = lax.broadcasted_iota(jnp.int32, weight_ref.shape[1:], 1)
    for q in range(weight_ref.shape[0]):
        frequency_id = q * bins + (column // bins) * half + column % half
        frequency = frequency_id.astype(jnp.float32)
        taper = jnp.clip((crossing - frequency) / taper_width + 0.5, 0.0, 1.0)
        weight_ref[q] = taper * jnp.where(frequency_id == 0, 1.0, 2.0) / samples
    group = 8
    pair = 2 * group
    depth = group * parts_of
    low_lanes = lax.broadcasted_iota(jnp.int32, (pair, bins), 1) < half
    dot = functools.partial(jnp.dot, preferred_element_type=jnp.float32)

    def make_block(b, carry):
        pltpu.make_async_copy(strain_rows(b), strain_buf.at[pl.ds(b * stretch, stretch)], strain_sem.at[b]).wait()
        moment = mechanism_ref[:, pl.ds(pl.multiple_of(b * block, block), block)]
        factors = jnp.transpose(jnp.concatenate([moment] * 4, axis=0)) * scale_ref[pl.ds(b, 1), :]
        head = factors.astype(jnp.bfloat16)
        tail = (factors - head.astype(jnp.float32)).astype(jnp.bfloat16)
        spread_rows = spread_ref[...].astype(jnp.bfloat16)
        wide = [dot(piece, spread_rows) for piece in (head, tail)]
        for first in range(0, block, pair):
            sums = []
            for start in (first, first + group):
                rows = []
                for piece in wide:
                    tile = piece[start : start + group]
                    twice = jnp.concatenate([tile, tile], axis=0).astype(jnp.bfloat16)
                    rows += [twice * own_ref[:pair], twice * own_ref[pair:]]
                product = dot(
                    jnp.concatenate(rows, axis=0),
                    strain_buf[pl.ds(pl.multiple_of(b * stretch + start * parts_of, depth), depth), :],
                )
                sums.append(product[: 2 * pair] + product[2 * pair :])
            quarters = [
                jnp.concatenate([part_sum[q * group : (q + 1) * group] for part_sum in sums], axis=0)
                for q in range(4)
            ]
            for c in range(2):
                real, imag = quarters[c], quarters[2 + c]
                real_turned = pltpu.roll(real, half, 1)
                imag_turned = pltpu.roll(imag, half, 1)
                lanes = pl.ds(c * bins, bins)
                pieces = (
                    (0, 0, real, imag_turned),
                    (0, 1, imag, -real_turned),
                    (1, 0, real_turned, imag),
                    (1, 1, imag_turned, -real),
                )
                for which, lower, first_half, second_half in pieces:
                    weights_ref[b, which, pl.ds(lower * block + first, pair), lanes] = jnp.where(
                        low_lanes, first_half, second_half
                    ).astype(jnp.bfloat16)
        return carry

    lax.fori_loop(0, blocks_here, make_block, 0)

    later = codes_ref.shape[0] - 1
    lowest = me * blocks_here

    def list_row(row, carry):
        seen, codes = carry[0], list(carry[1:])
        covered_here = covered_ref[row_ref[row]]
        found = jnp.int32(0)
        for slot in range(slot_total):
            local = blocks_ref[row_ref[row], slot] - lowest
            live = (slot < covered_here) & (local >= 0) & (local < blocks_here)
            code = (row * blocks_here + local) * blocks_here + found
            for j in range(later):
                codes[j] = jnp.where(live & (seen == j), code, codes[j])
            found = found + live.astype(jnp.int32)
            seen = seen + live.astype(jnp.int32)
        return (seen, *codes)

    seen, *codes = lax.fori_loop(
        0, slots_ref.shape[0], list_row, (jnp.int32(0),) + (jnp.int32(-1),) * later
    )
    for j, code in enumerate([seen] + codes):
        codes_ref[j] = jnp.full(codes_ref.shape[1:], code, jnp.int32)
    table_copy.wait()
    band_copy.wait()
    down = ((1,), (0,))
    lines = [pl.ds(pl.multiple_of(lax.rem(part + k, 2) * own, own), own) for k in range(2)]
    bands = [
        wide_dot(band_both[0], table_ref[q, 0, lines[0], :], table_ref[q, 1, lines[0], :], down)
        + wide_dot(band_both[1], table_ref[q, 0, lines[1], :], table_ref[q, 1, lines[1], :], down)
        for q in range(spectrum_ref.shape[0])
    ]
    for q, band in enumerate(bands):
        spectrum_ref[q] = band
    for copy in sends:
        copy.wait_send()
    for peer in peers:
        arrival = slots_ref.at[peer]
        pltpu.make_async_remote_copy(
            src_ref=arrival,
            dst_ref=arrival,
            send_sem=send_sem.at[0],
            recv_sem=recv_sem.at[peer],
            device_id={"pt": peer},
            device_id_type=MESH,
        ).wait_recv()


def turn(first, second):
    return (
        first[0] * second[0] - first[1] * second[1],
        first[0] * second[1] + first[1] * second[0],
    )


def quarter_unit(angle):
    off = angle - 0.25 * math.pi
    square = off * off
    sine = off * (
        1.0
        + square * (-1.0 / 6 + square * (1.0 / 120 + square * (-1.0 / 5040 + square * (1.0 / 362880))))
    )
    cosine = 1.0 + square * (
        -0.5
        + square
        * (1.0 / 24 + square * (-1.0 / 720 + square * (1.0 / 40320 + square * (-1.0 / 3628800))))
    )
    scale = math.sqrt(0.5)
    return scale * (cosine - sine), scale * (cosine + sine)


def slot_rows(slots_ref, row, found, spread):
    pieces = [
        slots_ref[row, found, h].astype(jnp.int32).astype(jnp.float32)
        for h in range(slots_ref.shape[2])
    ]
    onset = jnp.concatenate([piece[:spread] for piece in pieces], axis=0)
    slip = jnp.concatenate([piece[spread:] for piece in pieces], axis=0)
    return onset / onset_steps + onset_middle, slip / slip_steps


def with_sums(action):
    units = [pltpu.ACC(unit)((256, 256), jnp.float32) for unit in (0, 0, 1, 1)]
    pl.run_scoped(lambda *sums: action((sums[:2], sums[2:])), *units)


def pair_spectrum(step_angle, slots_ref, weights_ref, sums, row, found, local):
    halves, depth, columns = weights_ref.shape[1:]
    spread = slots_ref.shape[3] // 2
    bins = columns // 2
    half = bins // 2
    fine_total = 16
    reach = fine_total // 2
    onset, slip = slot_rows(slots_ref, row, found, spread)
    variations = onset.shape[0]
    powers = [None, quarter_unit(step_angle * onset)]
    for k in range(2, reach + 1):
        powers.append(turn(powers[k // 2], powers[k - k // 2]))
    leap = turn(powers[reach], powers[reach])
    far = leap
    for unused in range(int(math.log2(bins // fine_total))):
        far = turn(far, far)
    second_part = lax.axis_index("cmp") == 1
    centre = turn(
        powers[reach],
        (slip * jnp.where(second_part, far[0], 1.0), slip * jnp.where(second_part, far[1], 0.0)),
    )
    rounds = half // fine_total
    centres = [centre]
    for unused in range(halves * rounds - 1):
        centres.append(turn(centres[-1], leap))
    for which in range(halves):
        pltpu.matmul_push_rhs(weights_ref[local, which], 0, which)
    lane_bin = lax.broadcasted_iota(jnp.int32, (8, 128), 1) % half
    tiles = [
        [
            [jnp.zeros((8, 128), jnp.float32) for lane in range(columns // 128)]
            for line in range(variations // 8)
        ]
        for which in range(halves)
    ]

    def start(which, h):
        middle = centres[which * rounds + h]
        near = [None] * fine_total
        near[reach] = middle
        for k in range(1, reach + 1):
            cos_cos, sin_sin = middle[0] * powers[k][0], middle[1] * powers[k][1]
            sin_cos, cos_sin = middle[1] * powers[k][0], middle[0] * powers[k][1]
            near[reach - k] = (cos_cos + sin_sin, sin_cos - cos_sin)
            if k < reach:
                near[reach + k] = (cos_cos - sin_sin, sin_cos + cos_sin)
        pieces = [
            jnp.concatenate([phase[0].astype(jnp.bfloat16), phase[1].astype(jnp.bfloat16)], axis=1)
            for phase in near
        ]
        pltpu.matmul_acc_lhs(
            sums[which][h % 2], jnp.concatenate(pieces, axis=0), load_staged_rhs=0 if h == 0 else None
        )

    def finish(which, h):
        product = pltpu.matmul_pop(sums[which][h % 2])
        for k in range(fine_total):
            here = lane_bin == h * fine_total + k
            for line, across in enumerate(tiles[which]):
                first = k * variations + 8 * line
                for lane in range(len(across)):
                    across[lane] = jnp.where(
                        here, product[first : first + 8, 128 * lane : 128 * (lane + 1)], across[lane]
                    )

    for h in range(rounds + 1):
        for which in range(halves):
            if h < rounds:
                start(which, h)
            if h > 0:
                finish(which, h - 1)
    return [
        jnp.concatenate([jnp.concatenate(across, axis=1) for across in lines], axis=0)
        for lines in tiles
    ]


def pair_kernel(
    step_angle,
    row_hbm,
    blocks_hbm,
    covered_hbm,
    weights_ref,
    slots_ref,
    codes_ref,
    total_ref,
    row_ref,
    blocks_ref,
    covered_ref,
    load_sem,
):
    me = lax.axis_index("pt")
    blocks_here = weights_ref.shape[0]
    rows = slots_ref.shape[0]
    later = codes_ref.shape[0] - 1
    lowest = me * blocks_here

    @pl.when(codes_ref[0, 0, 0] > later)
    def _():
        loads = [
            pltpu.make_async_copy(source, target, load_sem.at[k])
            for k, (source, target) in enumerate(
                ((row_hbm, row_ref), (blocks_hbm, blocks_ref), (covered_hbm, covered_ref))
            )
        ]
        for copy in loads:
            copy.start()
        total_ref[...] = jnp.zeros_like(total_ref)
        for copy in loads:
            copy.wait()

        def one_row(row, seen):
            rupture = row_ref[row]

            def one_slot(slot, carry):
                found, seen = carry
                local = blocks_ref[rupture, slot] - lowest
                live = (local >= 0) & (local < blocks_here)

                def add(sums):
                    spectra = pair_spectrum(
                        step_angle, slots_ref, weights_ref, sums, row, found, local
                    )
                    for which, spectrum in enumerate(spectra):
                        total_ref[row, which] += spectrum

                @pl.when(live & (seen >= later))
                def _():
                    with_sums(add)

                return found + live.astype(jnp.int32), seen + live.astype(jnp.int32)

            return lax.fori_loop(0, covered_ref[rupture], one_slot, (jnp.int32(0), seen))[1]

        lax.fori_loop(0, rows, one_row, jnp.int32(0))


def merge_kernel(
    count,
    step_angle,
    begun_ref,
    codes_ref,
    slots_ref,
    weights_ref,
    weight_ref,
    spectrum_ref,
    band_ref,
    table_ref,
    out_ref,
    total_ref,
    partial_ref,
    arrived,
    send_sem,
    recv_sem,
):
    me = lax.axis_index("pt")
    part = lax.axis_index("cmp")
    blocks_here = weights_ref.shape[0]
    rows, halves, variations, columns = begun_ref.shape
    parts = weight_ref.shape[0]
    bins = columns // 2
    friends = []
    for peer in others(me, count):
        friends += [{"pt": peer, "cmp": 0}, {"pt": peer, "cmp": 1}]
    friends.append({"pt": me, "cmp": 1 - part})
    hail(friends)
    later = codes_ref.shape[0] - 1
    begun = codes_ref[0, 0, 0] > later
    total_ref[...] = jnp.where(begun, begun_ref[...], 0.0)

    def first_pairs(sums):
        for j in range(later):
            code = codes_ref[j + 1, 0, 0]
            safe = jnp.maximum(code, 0)
            holder = lax.div(safe, blocks_here)
            row = lax.div(holder, blocks_here)
            spectra = pair_spectrum(
                step_angle,
                slots_ref,
                weights_ref,
                sums,
                row,
                safe - holder * blocks_here,
                holder - row * blocks_here,
            )
            chosen = jnp.where(code < 0, -1, row)
            for other in range(rows):
                share = jnp.where(chosen == other, 1.0, 0.0)
                for which in range(halves):
                    total_ref[other, which] += share * spectra[which]

    with_sums(first_pairs)
    partial_ref[...] = total_ref[...].astype(partial_ref.dtype)
    await_all(friends)
    sends = []
    for step, friend in enumerate(friends):
        copy = pltpu.make_async_remote_copy(
            src_ref=partial_ref.at[friend["pt"]],
            dst_ref=arrived.at[me, part],
            send_sem=send_sem.at[step],
            recv_sem=recv_sem.at[me, part],
            device_id=friend,
            device_id_type=MESH,
        )
        copy.start()
        sends.append(copy)
    steps = pl.ds(pl.multiple_of(part * out_ref.shape[3], out_ref.shape[3]), out_ref.shape[3])

    def finish(sums):
        for q in range(parts):
            for fine in range(2):
                pltpu.matmul_push_rhs(table_ref[q, fine, steps, :], q, fine, transpose=True)
        arrived[me, part] = partial_ref[me]
        for friend in friends:
            arrival = arrived.at[friend["pt"], friend["cmp"]]
            pltpu.make_async_remote_copy(
                src_ref=arrival,
                dst_ref=arrival,
                send_sem=send_sem.at[0],
                recv_sem=recv_sem.at[friend["pt"], friend["cmp"]],
                device_id=friend,
                device_id_type=MESH,
            ).wait_recv()
        for q in range(parts):
            total = arrived[0, q].astype(jnp.float32)
            for source in range(1, count):
                total = total + arrived[source, q].astype(jnp.float32)
            excess = []
            for c in range(2):
                lanes = slice(c * bins, (c + 1) * bins)
                whole = jnp.concatenate([total[which][:, lanes] for which in range(halves)], axis=1)
                here = pl.ds(c * variations, variations)
                excess.append((whole - spectrum_ref[q, here, :]) * weight_ref[q])
            rows_here = jnp.concatenate(excess, axis=0)
            head = rows_here.astype(jnp.bfloat16)
            tail = (rows_here - head.astype(jnp.float32)).astype(jnp.bfloat16)
            pltpu.matmul_acc_lhs(sums[0], jnp.concatenate([head, tail], axis=0), load_staged_rhs=q)
            pltpu.matmul_acc_lhs(sums[1], head, load_staged_rhs=q)
        coarse = pltpu.matmul_pop(sums[0])
        depth = 2 * variations
        low = band_ref[0] + (coarse[:depth] + (coarse[depth:] + pltpu.matmul_pop(sums[1])))
        for c in range(2):
            out_ref[0, :, c, :] = low[c * variations : (c + 1) * variations]

    pl.run_scoped(
        lambda *sums: finish(sums),
        pltpu.ACC(0)((4 * variations, 256), jnp.float32),
        pltpu.ACC(1)((2 * variations, 256), jnp.float32),
    )
    for copy in sends:
        copy.wait_send()


def final_kernel(low_ref, out_ref):
    out_ref[...] = low_ref[...]


def stay(array):
    return pltpu.with_memory_space_constraint(array, VMEM)


def body(
    strain_green,
    green_scale,
    mechanism,
    slip_amplitude,
    onset_time,
    rupture_row,
    rupture_blocks,
    block_count,
    crossover,
    high_band,
):
    points, parts_of, bins = strain_green.shape
    blocks_here = green_scale.shape[0]
    block = points // blocks_here
    rows_here, variations, slots = slip_amplitude.shape
    count = lax.axis_size("pt")
    parts = lax.axis_size("cmp")
    own = high_band.shape[3]
    samples = own * parts
    rows = rows_here * count
    tables = jnp.asarray(basis_tables(bins, parts, samples))
    spread, own_terms = spread_tables(parts_of, mechanism.shape[0], 8)
    vmem = pl.BlockSpec(memory_space=VMEM)
    smem = pl.BlockSpec(memory_space=SMEM)
    anywhere = pl.BlockSpec(memory_space=pltpu.HBM)
    grant = 24 * 1024 * 1024
    later = 6
    step_angle = 2.0 * math.pi / samples
    share = (blocks_here, 2, variations, block)
    weights, slots_all, bands, table, weight, band_spectrum, codes = pl.pallas_call(
        functools.partial(gather_kernel, count),
        out_shape=(
            VMEM((blocks_here, 2, 2 * block, 2 * bins), jnp.bfloat16),
            VMEM((rows,) + share, jnp.int16),
            VMEM((2, 2 * variations, own), jnp.float32),
            VMEM(tables.shape, jnp.bfloat16),
            VMEM((parts, variations, 2 * bins), jnp.float32),
            VMEM((parts, 2 * variations, 2 * bins), jnp.float32),
            VMEM((later + 1, 8, 128), jnp.int32),
        ),
        in_specs=[anywhere] * 13,
        out_specs=(vmem,) * 7,
        scratch_shapes=[
            SMEM(rupture_row.shape, jnp.int32),
            SMEM(rupture_blocks.shape, jnp.int32),
            SMEM(block_count.shape, jnp.int32),
            SMEM(crossover.shape, jnp.int32),
            VMEM(spread.shape, jnp.float32),
            VMEM(own_terms.shape, jnp.bfloat16),
            VMEM(green_scale.shape, green_scale.dtype),
            VMEM(mechanism.shape, mechanism.dtype),
            VMEM(slip_amplitude.shape, slip_amplitude.dtype),
            VMEM(onset_time.shape, onset_time.dtype),
            VMEM(high_band.shape, high_band.dtype),
            VMEM((points * parts_of, bins), strain_green.dtype),
            VMEM((slots // block, 2, variations, block), jnp.int16),
            VMEM((count - 1,) + share, jnp.int16),
            pltpu.SemaphoreType.DMA,
            pltpu.SemaphoreType.DMA((11,)),
            pltpu.SemaphoreType.DMA((blocks_here,)),
            pltpu.SemaphoreType.DMA((count,)),
            pltpu.SemaphoreType.DMA((count + 1,)),
        ],
        compiler_params=pltpu.CompilerParams(collective_id=0, has_side_effects=True),
        name="gather",
    )(
        rupture_row,
        rupture_blocks,
        block_count,
        crossover,
        strain_green.reshape(points * parts_of, bins),
        green_scale,
        mechanism,
        slip_amplitude,
        onset_time,
        high_band,
        tables,
        jnp.asarray(spread),
        jnp.asarray(own_terms),
    )
    begun = pl.pallas_call(
        functools.partial(pair_kernel, step_angle),
        out_shape=VMEM((rows, 2, variations, 2 * bins), jnp.float32),
        in_specs=[anywhere] * 3 + [vmem] * 3,
        out_specs=vmem,
        scratch_shapes=[
            SMEM(rupture_row.shape, jnp.int32),
            SMEM(rupture_blocks.shape, jnp.int32),
            SMEM(block_count.shape, jnp.int32),
            pltpu.SemaphoreType.DMA((3,)),
        ],
        compiler_params=pltpu.CompilerParams(vmem_limit_bytes=grant),
        name="pairs",
    )(rupture_row, rupture_blocks, block_count, stay(weights), stay(slots_all), stay(codes))
    return pl.pallas_call(
        functools.partial(merge_kernel, count, step_angle),
        out_shape=jax.ShapeDtypeStruct(high_band.shape, high_band.dtype),
        in_specs=[vmem] * 8,
        out_specs=vmem,
        scratch_shapes=[
            VMEM((rows, 2, variations, 2 * bins), jnp.float32),
            VMEM((rows, 2, variations, 2 * bins), jnp.bfloat16),
            VMEM((count, parts, 2, variations, 2 * bins), jnp.bfloat16),
            pltpu.SemaphoreType.DMA((2 * count - 1,)),
            pltpu.SemaphoreType.DMA((count, parts)),
        ],
        compiler_params=pltpu.CompilerParams(collective_id=1, has_side_effects=True, vmem_limit_bytes=grant),
        name="merge",
    )(stay(begun), stay(codes), stay(slots_all), stay(weights), stay(weight), stay(band_spectrum), stay(bands), stay(table))


def solution(mesh):
    return jax.shard_map(
        body,
        mesh=mesh,
        in_specs=(
            P(("site", "pt"), None, "cmp"),
            P(("site", "pt"), None),
            P(None, "pt"),
            P("pt", "var", None),
            P("pt", "var", None),
            P(),
            P(),
            P(),
            P(),
            P(("site", "pt"), "var", None, "cmp"),
        ),
        out_specs=P(("site", "pt"), "var", None, "cmp"),
        check_vma=False,
    )
```

```python
import functools
import math

import jax
import jax.numpy as jnp
import numpy as np
from jax import lax
from jax.experimental import pallas as pl
from jax.experimental.pallas import tpu as pltpu
from jax.sharding import PartitionSpec as P

taper_width = 8.0
onset_middle = 64.0
onset_steps = 512.0
slip_steps = 1024.0
MESH = pl.DeviceIdType.MESH
VMEM = pltpu.VMEM
SMEM = pltpu.SMEM


def column_bins(bins_here):
    half = bins_here // 2
    column = np.arange(2 * bins_here)
    return (column // bins_here) * half + column % half, (column // half) % 2


def basis_tables(bins_here, parts, samples):
    bins, imaginary = column_bins(bins_here)
    time = np.arange(samples)[:, None]
    tables = []
    for part in range(parts):
        angle = ((part * bins_here + bins)[None, :] * time % samples) * (2.0 * math.pi / samples)
        tables.append(np.where(imaginary[None, :] == 1, -np.sin(angle), np.cos(angle)))
    exact = np.stack(tables)
    upper = exact.astype(jnp.bfloat16)
    lower = (exact - upper.astype(np.float64)).astype(jnp.bfloat16)
    return np.stack([upper, lower], axis=1)


def spread_tables(parts_of, terms, group):
    depth = group * parts_of
    column = np.arange(depth)
    spread = (np.arange(parts_of)[:, None] == column[None, :] % parts_of).astype(np.float32)
    quarter = np.arange(parts_of // terms * group)
    own_point = quarter[:, None] % group == column[None, :] // parts_of
    own_term = quarter[:, None] // group == (column[None, :] % parts_of) // terms
    return spread, (own_point & own_term).astype(jnp.bfloat16)


def wide_dot(rows, upper, lower, dims):
    head = rows.astype(jnp.bfloat16)
    tail = (rows - head.astype(jnp.float32)).astype(jnp.bfloat16)
    dot = functools.partial(
        lax.dot_general, dimension_numbers=(dims, ((), ())), preferred_element_type=jnp.float32
    )
    return dot(head, upper) + (dot(head, lower) + dot(tail, upper))


def hail(peers):
    barrier = pltpu.get_barrier_semaphore()
    for peer in peers:
        pl.semaphore_signal(barrier, inc=1, device_id=peer, device_id_type=MESH)


def await_all(peers):
    pl.semaphore_wait(pltpu.get_barrier_semaphore(), len(peers))


def greet(peers):
    hail(peers)
    await_all(peers)


def others(me, count):
    sense = jnp.where(2 * me < count, count - 1, 1)
    return [lax.rem(me + sense * step, count) for step in range(1, count)]


def gather_kernel(
    count,
    row_hbm,
    blocks_hbm,
    covered_hbm,
    crossover_hbm,
    strain_ref,
    scale_hbm,
    mechanism_hbm,
    slip_hbm,
    onset_hbm,
    band_hbm,
    table_hbm,
    spread_hbm,
    own_hbm,
    weights_ref,
    slots_ref,
    band_both,
    table_ref,
    weight_ref,
    spectrum_ref,
    codes_ref,
    row_ref,
    blocks_ref,
    covered_ref,
    crossover_ref,
    spread_ref,
    own_ref,
    scale_ref,
    mechanism_ref,
    slip_ref,
    onset_ref,
    band_ref,
    strain_buf,
    coded_ref,
    slot_pack,
    local_sem,
    load_sem,
    strain_sem,
    send_sem,
    recv_sem,
):
    me = lax.axis_index("pt")
    part = lax.axis_index("cmp")
    partner = {"cmp": 1 - part}
    blocks_here = scale_ref.shape[0]
    parts_of = scale_ref.shape[1]
    stretch = strain_ref.shape[0] // blocks_here
    block = stretch // parts_of
    bins = strain_ref.shape[1]
    half = bins // 2
    own = band_ref.shape[3]
    variations = band_ref.shape[1]
    samples = own * table_ref.shape[0]
    peers = others(me, count)
    friends = [{"pt": peer} for peer in peers] + [partner]
    hail(friends)
    loads = []
    for k, (source, target) in enumerate(
        (
            (row_hbm, row_ref),
            (blocks_hbm, blocks_ref),
            (covered_hbm, covered_ref),
            (slip_hbm, slip_ref),
            (onset_hbm, onset_ref),
            (band_hbm, band_ref),
            (mechanism_hbm, mechanism_ref),
            (scale_hbm, scale_ref),
            (spread_hbm, spread_ref),
            (own_hbm, own_ref),
            (crossover_hbm, crossover_ref),
        )
    ):
        copy = pltpu.make_async_copy(source, target, load_sem.at[k])
        copy.start()
        loads.append(copy)
    def strain_rows(b):
        return strain_ref.at[pl.ds(pl.multiple_of(b * stretch, stretch), stretch)]

    for b in range(blocks_here):
        pltpu.make_async_copy(strain_rows(b), strain_buf.at[pl.ds(b * stretch, stretch)], strain_sem.at[b]).start()
    table_copy = pltpu.make_async_copy(table_hbm, table_ref, local_sem)
    table_copy.start()
    for copy in loads[:3]:
        copy.wait()
    rupture = row_ref[me]
    covered = covered_ref[rupture]
    spread = variations // 2

    slot_total = blocks_ref.shape[1]

    def chosen(target):
        lowest = target * blocks_here
        slots = [jnp.int32(0)] * blocks_here
        found = jnp.int32(0)
        for slot in range(slot_total):
            named = blocks_ref[rupture, slot]
            live = (slot < covered) & (named >= lowest) & (named < lowest + blocks_here)
            for k in range(min(blocks_here, slot + 1)):
                slots[k] = jnp.where(live & (found == k), slot, slots[k])
            found = found + live.astype(jnp.int32)
        return slots

    sent = [chosen(peer) for peer in peers]
    kept = chosen(me)
    for copy in loads[3:5]:
        copy.wait()
    for slot in range(slot_total):
        lanes = pl.ds(slot * block, block)
        onset = (onset_ref[0, :, lanes] - onset_middle) * onset_steps
        onset = jnp.minimum(jnp.round(onset), onset_middle * onset_steps - 1.0)
        slip = slip_ref[0, :, lanes].astype(jnp.float32) * slip_steps
        for h in range(2):
            lines = slice(h * spread, (h + 1) * spread)
            coded_ref[slot, h] = (
                jnp.concatenate([onset[lines], slip[lines]], axis=0)
                .astype(jnp.int32)
                .astype(coded_ref.dtype)
            )

    for step, slots in enumerate(sent):
        for k, slot in enumerate(slots):
            slot_pack[step, k] = coded_ref[slot]
    await_all(friends)
    sends = []
    for step, peer in enumerate(peers):
        copy = pltpu.make_async_remote_copy(
            src_ref=slot_pack.at[step],
            dst_ref=slots_ref.at[me],
            send_sem=send_sem.at[step],
            recv_sem=recv_sem.at[me],
            device_id={"pt": peer},
            device_id_type=MESH,
        )
        copy.start()
        sends.append(copy)
    loads[5].wait()
    for c in range(2):
        band_both[0, pl.ds(c * variations, variations), :] = band_ref[0, :, c, :]
    band_copy = pltpu.make_async_remote_copy(
        src_ref=band_both.at[0],
        dst_ref=band_both.at[1],
        send_sem=send_sem.at[count - 1],
        recv_sem=recv_sem.at[count],
        device_id=partner,
        device_id_type=MESH,
    )
    band_copy.start()
    for k, slot in enumerate(kept):
        slots_ref[me, k] = coded_ref[slot]

    for copy in loads[6:]:
        copy.wait()
    crossing = crossover_ref[rupture].astype(jnp.float32)
    column = lax.broadcasted_iota(jnp.int32, weight_ref.shape[1:], 1)
    for q in range(weight_ref.shape[0]):
        frequency_id = q * bins + (column // bins) * half + column % half
        frequency = frequency_id.astype(jnp.float32)
        taper = jnp.clip((crossing - frequency) / taper_width + 0.5, 0.0, 1.0)
        weight_ref[q] = taper * jnp.where(frequency_id == 0, 1.0, 2.0) / samples
    group = 8
    pair = 2 * group
    depth = group * parts_of
    low_lanes = lax.broadcasted_iota(jnp.int32, (pair, bins), 1) < half
    dot = functools.partial(jnp.dot, preferred_element_type=jnp.float32)

    def make_block(b, carry):
        pltpu.make_async_copy(strain_rows(b), strain_buf.at[pl.ds(b * stretch, stretch)], strain_sem.at[b]).wait()
        moment = mechanism_ref[:, pl.ds(pl.multiple_of(b * block, block), block)]
        factors = jnp.transpose(jnp.concatenate([moment] * 4, axis=0)) * scale_ref[pl.ds(b, 1), :]
        head = factors.astype(jnp.bfloat16)
        tail = (factors - head.astype(jnp.float32)).astype(jnp.bfloat16)
        spread_rows = spread_ref[...].astype(jnp.bfloat16)
        wide = [dot(piece, spread_rows) for piece in (head, tail)]
        for first in range(0, block, pair):
            sums = []
            for start in (first, first + group):
                rows = []
                for piece in wide:
                    tile = piece[start : start + group]
                    twice = jnp.concatenate([tile, tile], axis=0).astype(jnp.bfloat16)
                    rows += [twice * own_ref[:pair], twice * own_ref[pair:]]
                product = dot(
                    jnp.concatenate(rows, axis=0),
                    strain_buf[pl.ds(pl.multiple_of(b * stretch + start * parts_of, depth), depth), :],
                )
                sums.append(product[: 2 * pair] + product[2 * pair :])
            quarters = [
                jnp.concatenate([part_sum[q * group : (q + 1) * group] for part_sum in sums], axis=0)
                for q in range(4)
            ]
            for c in range(2):
                real, imag = quarters[c], quarters[2 + c]
                real_turned = pltpu.roll(real, half, 1)
                imag_turned = pltpu.roll(imag, half, 1)
                lanes = pl.ds(c * bins, bins)
                pieces = (
                    (0, 0, real, imag_turned),
                    (0, 1, imag, -real_turned),
                    (1, 0, real_turned, imag),
                    (1, 1, imag_turned, -real),
                )
                for which, lower, first_half, second_half in pieces:
                    weights_ref[b, which, pl.ds(lower * block + first, pair), lanes] = jnp.where(
                        low_lanes, first_half, second_half
                    ).astype(jnp.bfloat16)
        return carry

    lax.fori_loop(0, blocks_here, make_block, 0)

    later = codes_ref.shape[0] - 1
    lowest = me * blocks_here

    def list_row(row, carry):
        seen, codes = carry[0], list(carry[1:])
        covered_here = covered_ref[row_ref[row]]
        found = jnp.int32(0)
        for slot in range(slot_total):
            local = blocks_ref[row_ref[row], slot] - lowest
            live = (slot < covered_here) & (local >= 0) & (local < blocks_here)
            code = (row * blocks_here + local) * blocks_here + found
            for j in range(later):
                codes[j] = jnp.where(live & (seen == j), code, codes[j])
            found = found + live.astype(jnp.int32)
            seen = seen + live.astype(jnp.int32)
        return (seen, *codes)

    seen, *codes = lax.fori_loop(
        0, slots_ref.shape[0], list_row, (jnp.int32(0),) + (jnp.int32(-1),) * later
    )
    for j, code in enumerate([seen] + codes):
        codes_ref[j] = jnp.full(codes_ref.shape[1:], code, jnp.int32)
    table_copy.wait()
    band_copy.wait()
    down = ((1,), (0,))
    lines = [pl.ds(pl.multiple_of(lax.rem(part + k, 2) * own, own), own) for k in range(2)]
    bands = [
        wide_dot(band_both[0], table_ref[q, 0, lines[0], :], table_ref[q, 1, lines[0], :], down)
        + wide_dot(band_both[1], table_ref[q, 0, lines[1], :], table_ref[q, 1, lines[1], :], down)
        for q in range(spectrum_ref.shape[0])
    ]
    for q, band in enumerate(bands):
        spectrum_ref[q] = band
    for copy in sends:
        copy.wait_send()
    for peer in peers:
        arrival = slots_ref.at[peer]
        pltpu.make_async_remote_copy(
            src_ref=arrival,
            dst_ref=arrival,
            send_sem=send_sem.at[0],
            recv_sem=recv_sem.at[peer],
            device_id={"pt": peer},
            device_id_type=MESH,
        ).wait_recv()


def turn(first, second):
    return (
        first[0] * second[0] - first[1] * second[1],
        first[0] * second[1] + first[1] * second[0],
    )


def quarter_unit(angle):
    off = angle - 0.25 * math.pi
    square = off * off
    sine = off * (
        1.0
        + square * (-1.0 / 6 + square * (1.0 / 120 + square * (-1.0 / 5040 + square * (1.0 / 362880))))
    )
    cosine = 1.0 + square * (
        -0.5
        + square
        * (1.0 / 24 + square * (-1.0 / 720 + square * (1.0 / 40320 + square * (-1.0 / 3628800))))
    )
    scale = math.sqrt(0.5)
    return scale * (cosine - sine), scale * (cosine + sine)


def slot_rows(slots_ref, row, found, spread):
    pieces = [
        slots_ref[row, found, h].astype(jnp.int32).astype(jnp.float32)
        for h in range(slots_ref.shape[2])
    ]
    onset = jnp.concatenate([piece[:spread] for piece in pieces], axis=0)
    slip = jnp.concatenate([piece[spread:] for piece in pieces], axis=0)
    return onset / onset_steps + onset_middle, slip / slip_steps


def with_sums(action):
    units = [pltpu.ACC(unit)((256, 256), jnp.float32) for unit in (0, 0, 1, 1)]
    pl.run_scoped(lambda *sums: action((sums[:2], sums[2:])), *units)


def pair_spectrum(step_angle, slots_ref, weights_ref, sums, found_ref, row, found, local):
    halves, depth, columns = weights_ref.shape[1:]
    spread = slots_ref.shape[3] // 2
    bins = columns // 2
    half = bins // 2
    fine_total = 16
    reach = fine_total // 2
    onset, slip = slot_rows(slots_ref, row, found, spread)
    variations = onset.shape[0]
    powers = [None, quarter_unit(step_angle * onset)]
    for k in range(2, reach + 1):
        powers.append(turn(powers[k // 2], powers[k - k // 2]))
    leap = turn(powers[reach], powers[reach])
    far = leap
    for unused in range(int(math.log2(bins // fine_total))):
        far = turn(far, far)
    second_part = lax.axis_index("cmp") == 1
    centre = turn(
        powers[reach],
        (slip * jnp.where(second_part, far[0], 1.0), slip * jnp.where(second_part, far[1], 0.0)),
    )
    rounds = half // fine_total
    centres = [centre]
    for unused in range(halves * rounds - 1):
        centres.append(turn(centres[-1], leap))
    for which in range(halves):
        pltpu.matmul_push_rhs(weights_ref[local, which], 0, which)
    lane_bin = lax.broadcasted_iota(jnp.int32, (8, 128), 1) % half
    tiles = [
        [
            [jnp.zeros((8, 128), jnp.float32) for lane in range(columns // 128)]
            for line in range(variations // 8)
        ]
        for which in range(halves)
    ]

    def start(which, h):
        middle = centres[which * rounds + h]
        near = [None] * fine_total
        near[reach] = middle
        for k in range(1, reach + 1):
            cos_cos, sin_sin = middle[0] * powers[k][0], middle[1] * powers[k][1]
            sin_cos, cos_sin = middle[1] * powers[k][0], middle[0] * powers[k][1]
            near[reach - k] = (cos_cos + sin_sin, sin_cos - cos_sin)
            if k < reach:
                near[reach + k] = (cos_cos - sin_sin, sin_cos + cos_sin)
        pieces = [
            jnp.concatenate([phase[0].astype(jnp.bfloat16), phase[1].astype(jnp.bfloat16)], axis=1)
            for phase in near
        ]
        pltpu.matmul_acc_lhs(
            sums[which][h % 2], jnp.concatenate(pieces, axis=0), load_staged_rhs=0 if h == 0 else None
        )

    def finish(which, h):
        product = pltpu.matmul_pop(sums[which][h % 2])
        for k in range(fine_total):
            here = lane_bin == h * fine_total + k
            for line, across in enumerate(tiles[which]):
                first = k * variations + 8 * line
                for lane in range(len(across)):
                    tile = product[first : first + 8, 128 * lane : 128 * (lane + 1)]
                    if lane == 0:
                        across[lane] = jnp.where(here, tile, across[lane])
                    else:
                        pltpu.store(
                            found_ref.at[which, pl.ds(8 * line, 8), pl.ds(128 * lane, 128)], tile, mask=here
                        )

    for h in range(rounds + 1):
        for which in range(halves):
            if h < rounds:
                start(which, h)
            if h > 0:
                finish(which, h - 1)
    return [
        jnp.concatenate(
            [jnp.concatenate([lines[0][0], found_ref[which, 0:8, 128:]], axis=1),
             jnp.concatenate([lines[1][0], found_ref[which, 8:16, 128:]], axis=1)], axis=0)
        for which, lines in enumerate(tiles)
    ]


def pair_kernel(
    step_angle,
    row_hbm,
    blocks_hbm,
    covered_hbm,
    weights_ref,
    slots_ref,
    codes_ref,
    total_ref,
    row_ref,
    blocks_ref,
    covered_ref,
    load_sem,
    found_ref,
):
    me = lax.axis_index("pt")
    blocks_here = weights_ref.shape[0]
    rows = slots_ref.shape[0]
    later = codes_ref.shape[0] - 1
    lowest = me * blocks_here

    @pl.when(codes_ref[0, 0, 0] > later)
    def _():
        loads = [
            pltpu.make_async_copy(source, target, load_sem.at[k])
            for k, (source, target) in enumerate(
                ((row_hbm, row_ref), (blocks_hbm, blocks_ref), (covered_hbm, covered_ref))
            )
        ]
        for copy in loads:
            copy.start()
        total_ref[...] = jnp.zeros_like(total_ref)
        for copy in loads:
            copy.wait()

        def one_row(row, seen):
            rupture = row_ref[row]

            def one_slot(slot, carry):
                found, seen = carry
                local = blocks_ref[rupture, slot] - lowest
                live = (local >= 0) & (local < blocks_here)

                def add(sums):
                    spectra = pair_spectrum(
                        step_angle, slots_ref, weights_ref, sums, found_ref, row, found, local
                    )
                    for which, spectrum in enumerate(spectra):
                        total_ref[row, which] += spectrum

                @pl.when(live & (seen >= later))
                def _():
                    with_sums(add)

                return found + live.astype(jnp.int32), seen + live.astype(jnp.int32)

            return lax.fori_loop(0, covered_ref[rupture], one_slot, (jnp.int32(0), seen))[1]

        lax.fori_loop(0, rows, one_row, jnp.int32(0))


def merge_kernel(
    count,
    step_angle,
    begun_ref,
    codes_ref,
    slots_ref,
    weights_ref,
    weight_ref,
    spectrum_ref,
    band_ref,
    table_ref,
    out_ref,
    total_ref,
    partial_ref,
    arrived,
    send_sem,
    recv_sem,
    found_ref,
):
    me = lax.axis_index("pt")
    part = lax.axis_index("cmp")
    blocks_here = weights_ref.shape[0]
    rows, halves, variations, columns = begun_ref.shape
    parts = weight_ref.shape[0]
    bins = columns // 2
    friends = []
    for peer in others(me, count):
        friends += [{"pt": peer, "cmp": 0}, {"pt": peer, "cmp": 1}]
    friends.append({"pt": me, "cmp": 1 - part})
    hail(friends)
    later = codes_ref.shape[0] - 1
    begun = codes_ref[0, 0, 0] > later
    total_ref[...] = jnp.where(begun, begun_ref[...], 0.0)

    def first_pairs(sums):
        for j in range(later):
            code = codes_ref[j + 1, 0, 0]
            safe = jnp.maximum(code, 0)
            holder = lax.div(safe, blocks_here)
            row = lax.div(holder, blocks_here)
            spectra = pair_spectrum(
                step_angle,
                slots_ref,
                weights_ref,
                sums,
                found_ref.at[j],
                row,
                safe - holder * blocks_here,
                holder - row * blocks_here,
            )
            chosen = jnp.where(code < 0, -1, row)
            for other in range(rows):
                share = jnp.where(chosen == other, 1.0, 0.0)
                for which in range(halves):
                    total_ref[other, which] += share * spectra[which]

    with_sums(first_pairs)
    partial_ref[...] = total_ref[...].astype(partial_ref.dtype)
    await_all(friends)
    sends = []
    for step, friend in enumerate(friends):
        copy = pltpu.make_async_remote_copy(
            src_ref=partial_ref.at[friend["pt"]],
            dst_ref=arrived.at[me, part],
            send_sem=send_sem.at[step],
            recv_sem=recv_sem.at[me, part],
            device_id=friend,
            device_id_type=MESH,
        )
        copy.start()
        sends.append(copy)
    steps = pl.ds(pl.multiple_of(part * out_ref.shape[3], out_ref.shape[3]), out_ref.shape[3])

    def finish(sums):
        for q in range(parts):
            for fine in range(2):
                pltpu.matmul_push_rhs(table_ref[q, fine, steps, :], q, fine, transpose=True)
        arrived[me, part] = partial_ref[me]
        for friend in friends:
            arrival = arrived.at[friend["pt"], friend["cmp"]]
            pltpu.make_async_remote_copy(
                src_ref=arrival,
                dst_ref=arrival,
                send_sem=send_sem.at[0],
                recv_sem=recv_sem.at[friend["pt"], friend["cmp"]],
                device_id=friend,
                device_id_type=MESH,
            ).wait_recv()
        for q in range(parts):
            total = arrived[0, q].astype(jnp.float32)
            for source in range(1, count):
                total = total + arrived[source, q].astype(jnp.float32)
            excess = []
            for c in range(2):
                lanes = slice(c * bins, (c + 1) * bins)
                whole = jnp.concatenate([total[which][:, lanes] for which in range(halves)], axis=1)
                here = pl.ds(c * variations, variations)
                excess.append((whole - spectrum_ref[q, here, :]) * weight_ref[q])
            rows_here = jnp.concatenate(excess, axis=0)
            head = rows_here.astype(jnp.bfloat16)
            tail = (rows_here - head.astype(jnp.float32)).astype(jnp.bfloat16)
            pltpu.matmul_acc_lhs(sums[0], jnp.concatenate([head, tail], axis=0), load_staged_rhs=q)
            pltpu.matmul_acc_lhs(sums[1], head, load_staged_rhs=q)
        coarse = pltpu.matmul_pop(sums[0])
        depth = 2 * variations
        low = band_ref[0] + (coarse[:depth] + (coarse[depth:] + pltpu.matmul_pop(sums[1])))
        for c in range(2):
            out_ref[0, :, c, :] = low[c * variations : (c + 1) * variations]

    pl.run_scoped(
        lambda *sums: finish(sums),
        pltpu.ACC(0)((4 * variations, 256), jnp.float32),
        pltpu.ACC(1)((2 * variations, 256), jnp.float32),
    )
    for copy in sends:
        copy.wait_send()


def final_kernel(low_ref, out_ref):
    out_ref[...] = low_ref[...]


def stay(array):
    return pltpu.with_memory_space_constraint(array, VMEM)


def body(
    strain_green,
    green_scale,
    mechanism,
    slip_amplitude,
    onset_time,
    rupture_row,
    rupture_blocks,
    block_count,
    crossover,
    high_band,
):
    points, parts_of, bins = strain_green.shape
    blocks_here = green_scale.shape[0]
    block = points // blocks_here
    rows_here, variations, slots = slip_amplitude.shape
    count = lax.axis_size("pt")
    parts = lax.axis_size("cmp")
    own = high_band.shape[3]
    samples = own * parts
    rows = rows_here * count
    tables = jnp.asarray(basis_tables(bins, parts, samples))
    spread, own_terms = spread_tables(parts_of, mechanism.shape[0], 8)
    vmem = pl.BlockSpec(memory_space=VMEM)
    smem = pl.BlockSpec(memory_space=SMEM)
    anywhere = pl.BlockSpec(memory_space=pltpu.HBM)
    grant = 24 * 1024 * 1024
    later = 6
    step_angle = 2.0 * math.pi / samples
    share = (blocks_here, 2, variations, block)
    weights, slots_all, bands, table, weight, band_spectrum, codes = pl.pallas_call(
        functools.partial(gather_kernel, count),
        out_shape=(
            VMEM((blocks_here, 2, 2 * block, 2 * bins), jnp.bfloat16),
            VMEM((rows,) + share, jnp.int16),
            VMEM((2, 2 * variations, own), jnp.float32),
            VMEM(tables.shape, jnp.bfloat16),
            VMEM((parts, variations, 2 * bins), jnp.float32),
            VMEM((parts, 2 * variations, 2 * bins), jnp.float32),
            VMEM((later + 1, 8, 128), jnp.int32),
        ),
        in_specs=[anywhere] * 13,
        out_specs=(vmem,) * 7,
        scratch_shapes=[
            SMEM(rupture_row.shape, jnp.int32),
            SMEM(rupture_blocks.shape, jnp.int32),
            SMEM(block_count.shape, jnp.int32),
            SMEM(crossover.shape, jnp.int32),
            VMEM(spread.shape, jnp.float32),
            VMEM(own_terms.shape, jnp.bfloat16),
            VMEM(green_scale.shape, green_scale.dtype),
            VMEM(mechanism.shape, mechanism.dtype),
            VMEM(slip_amplitude.shape, slip_amplitude.dtype),
            VMEM(onset_time.shape, onset_time.dtype),
            VMEM(high_band.shape, high_band.dtype),
            VMEM((points * parts_of, bins), strain_green.dtype),
            VMEM((slots // block, 2, variations, block), jnp.int16),
            VMEM((count - 1,) + share, jnp.int16),
            pltpu.SemaphoreType.DMA,
            pltpu.SemaphoreType.DMA((11,)),
            pltpu.SemaphoreType.DMA((blocks_here,)),
            pltpu.SemaphoreType.DMA((count,)),
            pltpu.SemaphoreType.DMA((count + 1,)),
        ],
        compiler_params=pltpu.CompilerParams(collective_id=0, has_side_effects=True),
        name="gather",
    )(
        rupture_row,
        rupture_blocks,
        block_count,
        crossover,
        strain_green.reshape(points * parts_of, bins),
        green_scale,
        mechanism,
        slip_amplitude,
        onset_time,
        high_band,
        tables,
        jnp.asarray(spread),
        jnp.asarray(own_terms),
    )
    begun = pl.pallas_call(
        functools.partial(pair_kernel, step_angle),
        out_shape=VMEM((rows, 2, variations, 2 * bins), jnp.float32),
        in_specs=[anywhere] * 3 + [vmem] * 3,
        out_specs=vmem,
        scratch_shapes=[
            SMEM(rupture_row.shape, jnp.int32),
            SMEM(rupture_blocks.shape, jnp.int32),
            SMEM(block_count.shape, jnp.int32),
            pltpu.SemaphoreType.DMA((3,)),
            VMEM((2, variations, 2 * bins), jnp.float32),
        ],
        compiler_params=pltpu.CompilerParams(vmem_limit_bytes=grant),
        name="pairs",
    )(rupture_row, rupture_blocks, block_count, stay(weights), stay(slots_all), stay(codes))
    return pl.pallas_call(
        functools.partial(merge_kernel, count, step_angle),
        out_shape=jax.ShapeDtypeStruct(high_band.shape, high_band.dtype),
        in_specs=[vmem] * 8,
        out_specs=vmem,
        scratch_shapes=[
            VMEM((rows, 2, variations, 2 * bins), jnp.float32),
            VMEM((rows, 2, variations, 2 * bins), jnp.bfloat16),
            VMEM((count, parts, 2, variations, 2 * bins), jnp.bfloat16),
            pltpu.SemaphoreType.DMA((2 * count - 1,)),
            pltpu.SemaphoreType.DMA((count, parts)),
            VMEM((later, 2, variations, 2 * bins), jnp.float32),
        ],
        compiler_params=pltpu.CompilerParams(collective_id=1, has_side_effects=True, vmem_limit_bytes=grant),
        name="merge",
    )(stay(begun), stay(codes), stay(slots_all), stay(weights), stay(weight), stay(band_spectrum), stay(bands), stay(table))


def solution(mesh):
    return jax.shard_map(
        body,
        mesh=mesh,
        in_specs=(
            P(("site", "pt"), None, "cmp"),
            P(("site", "pt"), None),
            P(None, "pt"),
            P("pt", "var", None),
            P("pt", "var", None),
            P(),
            P(),
            P(),
            P(),
            P(("site", "pt"), "var", None, "cmp"),
        ),
        out_specs=P(("site", "pt"), "var", None, "cmp"),
        check_vma=False,
    )
```
